32 devices in a mesh: lat: 4 (over y, x), lon: 8 (over z, core).
Axes of the slice: x: 2, y: 2, z: 4, core: 2. Of those that a mesh axis runs over, the one named last changes fastest.
Arguments:
- members: float32 [80, 2, 256, 1024], P('lon', None, 'lat'), may hold values from -6 to 6
- obs_row: int32 [2, 4, 8, 64], P(None, 'lat', 'lon'), may hold values from 0 to 63
- obs_col: int32 [2, 4, 8, 64], P(None, 'lat', 'lon'), may hold values from 0 to 127
- obs_value: float32 [2, 4, 8, 64], P(None, 'lat', 'lon'), may hold values from -6 to 6
- obs_error: float32 [2, 4, 8, 64], P(None, 'lat', 'lon'), may hold values from 0.25 to 4
- obs_weight: float32 [2, 4, 8, 2, 64], P(None, 'lat', 'lon'), may hold values from 0.2 to 1
- obs_count: int32 [2, 4, 8], P(None, 'lat', 'lon'), may hold values from 8 to 64, as said below
Outputs:
- analysis: float32 [80, 2, 256, 1024], P('lon', None, 'lat')
The draws below stay inside these ranges and needn't reach their ends.
Inputs may be any that keep to these rules, and one draw needn't show every extreme that they name: The first obs_count slots of a tile hold its observations, the others are ignored; in each batch one tile holds 64. `obs_row`: row inside the owning tile. `obs_col`: column inside the owning tile.
All inputs are finite; a program needn't handle non-finite values.
Results may differ from the reference program's by a relative error of at most 0.0001.
Values sent between devices are 32-bit elements; how exact they have to be, the bound alone decides.
A program may use at most 192 MiB of HBM per device.

```python
import math
import jax
import jax.numpy as jnp
from jax import lax

K = 80
LEV = 2
CLAT = 64
CLON = 128
SLOTS = 64
NBATCH = 2
RAD = 48
BANDS = 4
SECTORS = 8
NLAT = 256
NLON = 1024


def draw_obs_count(key, part):
    low = max(SLOTS // 8, 1)
    first, second = jax.random.split(jax.random.fold_in(key, 17))
    tiles = BANDS * SECTORS
    counts = jax.random.randint(first, (NBATCH, tiles), low, SLOTS - low + 1)
    full_at = jax.random.randint(second, (NBATCH, 1), 0, tiles)
    counts = jnp.where(jnp.arange(tiles)[None, :] == full_at, SLOTS, counts)
    return counts.reshape(NBATCH, BANDS, SECTORS).astype(jnp.int32)


def plant(entries, own_key, low, largest):
    spot = [jax.random.randint(jax.random.fold_in(own_key, axis), (), 0, length) for axis, length in enumerate(entries.shape)]
    longest = entries.shape.index(max(entries.shape))
    next_to = spot[:longest] + [(spot[longest] + 1) % entries.shape[longest]] + spot[longest + 1:]
    return entries.at[tuple(spot)].set(low).at[tuple(next_to)].set(largest)


def shard_levels(key, dims, cuts, low, largest):
    def one(position, parts):
        steps = jax.random.uniform(jax.random.fold_in(jax.random.fold_in(key, 6), position), (parts,), jnp.float32, low / len(cuts), largest / len(cuts))
        return jnp.repeat(jnp.exp(steps), dims[position] // parts).reshape((-1,) + (1,) * (len(dims) - position - 1))

    level = one(*cuts[0])
    for cut in cuts[1:]:
        level = level * one(*cut)
    return level


def bell_draw(key, dims, scale, most, cuts=(), dtype=jnp.bfloat16):
    result = jax.random.normal(key, dims, jnp.float32) * scale
    if len(cuts) > 0:
        result = shard_levels(key, dims, cuts, -0.22, 0.18) * result
    return jnp.clip(result, min=-most, max=most).astype(dtype)


def setup_inputs(seed: int = 0) -> dict:
    seeds = jax.random.split(jax.random.key(seed), 8)
    members = bell_draw(seeds[0], (K, LEV, NLAT, NLON), 1.0, 6.0, ((0, 8), (2, 4)), jnp.float32)
    obs_row = plant(jax.random.randint(seeds[1], (NBATCH, BANDS, SECTORS, SLOTS), 0, CLAT), jax.random.fold_in(seeds[1], 1), 0, CLAT - 1).astype(jnp.int32)
    obs_col = plant(jax.random.randint(seeds[2], (NBATCH, BANDS, SECTORS, SLOTS), 0, CLON), jax.random.fold_in(seeds[2], 1), 0, CLON - 1).astype(jnp.int32)
    obs_value = bell_draw(seeds[3], (NBATCH, BANDS, SECTORS, SLOTS), 1.5, 6.0, ((1, 4), (2, 8)), jnp.float32)
    obs_error = jnp.clip(jnp.exp(math.log(4.0) - 2.7725887 * jax.random.uniform(seeds[4], (NBATCH, BANDS, SECTORS, SLOTS), jnp.float32) ** shard_levels(seeds[4], (NBATCH, BANDS, SECTORS, SLOTS), ((1, 4), (2, 8)), -0.2, 0.2)), 0.25, 4.0)
    obs_weight = jnp.clip(0.2 + 0.8 * jax.random.uniform(seeds[5], (NBATCH, BANDS, SECTORS, LEV, SLOTS), jnp.float32) ** shard_levels(seeds[5], (NBATCH, BANDS, SECTORS, LEV, SLOTS), ((1, 4), (2, 8)), -0.2, 0.2), 0.2, 1.0)
    obs_count = draw_obs_count(jax.random.fold_in(seeds[7], 71), 0)
    return {"members": members, "obs_row": obs_row, "obs_col": obs_col, "obs_value": obs_value, "obs_error": obs_error, "obs_weight": obs_weight, "obs_count": obs_count}


def gaspari(dist):
    z = dist / (0.5 * RAD)
    near = (((-0.25 * z + 0.5) * z + 0.625) * z - 5.0 / 3.0) * z * z + 1.0
    zfar = jnp.maximum(z, 1.0)
    far = ((((zfar / 12.0 - 0.5) * zfar + 0.625) * zfar + 5.0 / 3.0) * zfar - 5.0) * zfar + 4.0 - 2.0 / (3.0 * zfar)
    return jnp.where(z <= 1.0, near, jnp.where(z < 2.0, far, 0.0))

def reference(members, obs_row, obs_col, obs_value, obs_error, obs_weight, obs_count):
    state = members
    width = 2 * RAD + 1
    offsets = jnp.arange(-RAD, RAD + 1).astype(jnp.float32)
    taper_tab = gaspari(jnp.sqrt(offsets[:, None] ** 2 + offsets[None, :] ** 2))
    lat_base = (jnp.arange(BANDS) * CLAT).astype(jnp.int32)[:, None, None]
    lon_base = (jnp.arange(SECTORS) * CLON).astype(jnp.int32)[None, :, None]
    slot_ids = jnp.arange(SLOTS).astype(jnp.int32)[None, None, :]
    zero = jnp.zeros((), jnp.int32)
    for batch in range(NBATCH):
        glat = (obs_row[batch] + lat_base).reshape(-1).astype(jnp.int32)
        glon = (obs_col[batch] + lon_base).reshape(-1).astype(jnp.int32)
        weight = jnp.transpose(obs_weight[batch], (0, 1, 3, 2)).reshape(-1, LEV)
        valid = (slot_ids < obs_count[batch][:, :, None]).reshape(-1).astype(jnp.float32)
        err = obs_error[batch].reshape(-1)
        value = obs_value[batch].reshape(-1)
        picked = state[:, :, glat, glon]
        prior = jnp.einsum('klo,ol->ko', picked, weight, precision=lax.Precision.HIGHEST)
        prior_mean = lax.optimization_barrier(jnp.mean(prior, axis=0))
        prior_pert = prior - prior_mean
        spread = lax.optimization_barrier(jnp.sum(prior_pert * prior_pert, axis=0)) / (K - 1.0)
        denom = spread + err
        mean_coef = valid * (value - prior_mean) / denom
        pert_coef = valid / (denom * (1.0 + jnp.sqrt(err / denom)))
        mean = lax.optimization_barrier(jnp.mean(state, axis=0))
        pert = state - mean
        padded = jnp.pad(pert, ((0, 0), (0, 0), (RAD, RAD), (0, 0)))
        padded = jnp.concatenate([padded[..., NLON - RAD:], padded, padded[..., :RAD]], axis=-1)
        start = jnp.zeros(padded.shape, jnp.float32)

        def add_one(total, item):
            row, col, deviation, cmean, cpert = item
            window = lax.dynamic_slice(padded, (zero, zero, row, col), (K, LEV, width, width))
            cov = jnp.einsum('klyx,k->lyx', window, deviation, precision=lax.Precision.HIGHEST) / (K - 1.0)
            gain = cov * taper_tab
            coef = cmean - cpert * deviation
            delta = gain[None] * coef[:, None, None, None]
            current = lax.dynamic_slice(total, (zero, zero, row, col), (K, LEV, width, width))
            return (lax.dynamic_update_slice(total, current + delta, (zero, zero, row, col)), None)
        total, _ = lax.scan(add_one, start, (glat, glon, prior_pert.T, mean_coef, pert_coef))
        core = total[:, :, RAD:RAD + NLAT, :]
        inner = core[..., RAD:RAD + NLON]
        inner = inner.at[..., :RAD].add(core[..., RAD + NLON:])
        inner = inner.at[..., NLON - RAD:].add(core[..., :RAD])
        state = state + inner
    return state
```

```python
import functools

import jax
import jax.numpy as jnp
from jax import lax
from jax.experimental import pallas as pl
from jax.experimental.pallas import tpu as pltpu
from jax.sharding import PartitionSpec as P

NBATCH = 2
RAD = 48
STEP = 8
LANES = 128
HIGHEST = lax.Precision.HIGHEST
MESH = pl.DeviceIdType.MESH
AROUND = [(da, db) for da in (-1, 0, 1) for db in (-1, 0, 1) if (da, db) != (0, 0)]


def gaspari_sq(dist_sq):
    inverse = lax.rsqrt(jnp.maximum(dist_sq, 1e-12))
    z = dist_sq * inverse * (2.0 / RAD)
    near = (((-0.25 * z + 0.5) * z + 0.625) * z - 5.0 / 3.0) * (z * z) + 1.0
    far = (
        ((((z * (1.0 / 12.0) - 0.5) * z + 0.625) * z + 5.0 / 3.0) * z - 5.0) * z
        + 4.0
        - inverse * (RAD / 3.0)
    )
    return jnp.where(z <= 1.0, near, jnp.where(z < 2.0, far, 0.0))


def split(value):
    high = value.astype(jnp.bfloat16)
    low = (value - high.astype(jnp.float32)).astype(jnp.bfloat16)
    return high, low


def wrapped(gap, nlon):
    half = 0.5 * nlon
    return jnp.where(gap >= half, gap - nlon, jnp.where(gap < -half, gap + nlon, gap))


def fused_kernel(
    bands, parts, slots, info_ref, members_ref, out_ref,
    mem, state, info_all, pick, prior_parts, prior, cross, pack, packed, table, coef_t,
    lats, gaps, priors, coefs, coefs_high,
    in_send, in_recv, out_send, out_recv, info_send, info_recv, pick_send, pick_recv, near_send, near_recv, own_sem,
):
    group, levels, clat, nlon = members_ref.shape
    full = group * parts
    clon = nlon // parts
    pieces = clat // STEP
    third = 3 * slots
    total = 3 * third
    mine = full
    band = lax.axis_index("lat")
    me = lax.axis_index("lon")
    lat_first = (band * clat).astype(jnp.float32)
    lon_first = (me * clon).astype(jnp.float32)

    def to(d):
        return lax.rem(me + d, parts)

    def columns(sector):
        return pl.ds(pl.multiple_of(sector * clon, clon), clon)

    def rows_of(p):
        return pl.ds(pl.multiple_of(p * STEP, STEP), STEP)

    def inward(p, d):
        return pltpu.make_async_remote_copy(
            src_ref=members_ref.at[:, :, rows_of(p), columns(to(d))],
            dst_ref=state.at[pl.ds(me * group, group), :, rows_of(p), :],
            send_sem=in_send.at[p, d],
            recv_sem=in_recv.at[p, d],
            device_id={"lon": to(d)},
            device_id_type=MESH,
        )

    def outward(p, d):
        return pltpu.make_async_remote_copy(
            src_ref=state.at[pl.ds(to(d) * group, group), :, rows_of(p), :],
            dst_ref=out_ref.at[:, :, rows_of(p), columns(me)],
            send_sem=out_send.at[p, d],
            recv_sem=out_recv.at[p, d],
            device_id={"lon": to(d)},
            device_id_type=MESH,
        )

    def kept(p):
        return pltpu.make_async_copy(
            state.at[pl.ds(me * group, group), :, rows_of(p), :],
            out_ref.at[:, :, rows_of(p), columns(me)],
            own_sem.at[p],
        )

    def informing(d):
        return pltpu.make_async_remote_copy(
            src_ref=info_ref,
            dst_ref=info_all.at[me],
            send_sem=info_send.at[d],
            recv_sem=info_recv.at[d],
            device_id={"lon": to(d)},
            device_id_type=MESH,
        )

    def picking(d):
        return pltpu.make_async_remote_copy(
            src_ref=pick.at[to(d)],
            dst_ref=prior_parts.at[me],
            send_sem=pick_send.at[d],
            recv_sem=pick_recv.at[d],
            device_id={"lon": to(d)},
            device_id_type=MESH,
        )

    def sharing(batch, i):
        da, db = AROUND[i]
        spot = (1 - da) * 3 + 1 - db
        return pltpu.make_async_remote_copy(
            src_ref=packed.at[batch, pl.ds(batch * slots, slots), :],
            dst_ref=table.at[batch, pl.ds(spot * slots, slots), :],
            send_sem=near_send.at[batch, i],
            recv_sem=near_recv.at[batch, i],
            device_id={"lat": lax.rem(band + da + bands, bands), "lon": lax.rem(me + db + parts, parts)},
            device_id_type=MESH,
        )

    whole = pltpu.make_async_copy(members_ref, mem, own_sem.at[pieces])
    whole.start()
    own = pltpu.make_async_copy(
        members_ref.at[:, :, :, columns(me)], state.at[pl.ds(me * group, group)], own_sem.at[pieces + 1]
    )
    own.start()

    barrier = pltpu.get_barrier_semaphore()
    for d in range(1, parts):
        pl.semaphore_signal(barrier, inc=1, device_id={"lon": to(d)}, device_id_type=MESH)
    for da, db in AROUND:
        if da != 0:
            pl.semaphore_signal(
                barrier,
                inc=1,
                device_id={"lat": lax.rem(band + da + bands, bands), "lon": lax.rem(me + db + parts, parts)},
                device_id_type=MESH,
            )
    pl.semaphore_wait(barrier, parts - 1 + 6)

    for d in range(1, parts):
        informing(d).start()

    def send_in(p, carry):
        for d in range(1, parts):
            inward(p, d).start()
        return carry

    lax.fori_loop(0, pieces, send_in, 0)

    for d in range(1, parts):
        informing(d).wait()
    info_all[me] = info_ref[...]
    whole.wait()
    cell = lax.broadcasted_iota(jnp.int32, (clon, LANES), 0).astype(jnp.float32)
    grid_row = lax.broadcasted_iota(jnp.int32, (clat, LANES), 0).astype(jnp.float32)

    def pick_for(sector):
        about = info_all[sector]
        hot = jnp.where(cell == about[1:2], 1.0, 0.0).astype(jnp.bfloat16)
        chosen = grid_row == about[0:1]
        weight = jnp.stack([jnp.where(chosen, about[4 + l : 5 + l], 0.0) for l in range(levels)], axis=0)
        for k in range(group):
            values = mem[k, :, :, columns(sector)].reshape(levels * clat, clon)
            high, low = split(values)
            rest = values - high.astype(jnp.float32) - low.astype(jnp.float32)
            found = jnp.dot(
                jnp.concatenate([high, low, rest.astype(jnp.bfloat16)], axis=1),
                jnp.concatenate([hot, hot, hot], axis=0),
                preferred_element_type=jnp.float32,
            ).reshape(levels, clat, LANES)
            pick[sector, k : k + 1, :] = jnp.sum(
                jnp.sum(found * weight, axis=0), axis=0, keepdims=True
            )

    def pick_other(d, carry):
        pick_for(to(d))
        picking(d).start()
        return carry

    lax.fori_loop(1, parts, pick_other, 0)
    pick_for(me)
    prior_parts[me] = pick[me]
    for d in range(1, parts):
        picking(d).wait()
    for i in range(parts):
        prior[i * group : (i + 1) * group, :] = prior_parts[i]

    cross[...] = jnp.zeros_like(cross)
    pack[...] = jnp.zeros_like(pack)
    for batch in range(NBATCH):
        table[batch, total:, :] = jnp.zeros((table.shape[1] - total, LANES), jnp.float32)
    own_lat = lat_first + info_ref[0:1, :]
    own_lon = lon_first + info_ref[1:2, :]

    def share(batch):
        points = prior[...]
        mean = jnp.mean(points, axis=0, keepdims=True)
        pert = points - mean
        spread = jnp.sum(pert * pert, axis=0, keepdims=True) / (full - 1.0)
        err = info_ref[3:4, :]
        valid = info_ref[6:7, :]
        denom = spread + err
        pack[:full, :] = pert
        pack[mine : mine + 1, :] = valid * (info_ref[2:3, :] - mean) / denom
        pack[mine + 1 : mine + 2, :] = valid / (denom * (1.0 + jnp.sqrt(err / denom)))
        pack[mine + 2 : mine + 3, :] = own_lat
        pack[mine + 3 : mine + 4, :] = own_lon
        if batch == 0:
            cross[:full, :] = pert
        packed[batch] = pack[...].T
        for i in range(len(AROUND)):
            sharing(batch, i).start()
        table[batch, 4 * slots : 5 * slots, :] = packed[batch, batch * slots : (batch + 1) * slots, :]
        for i in range(len(AROUND)):
            sharing(batch, i).wait()

    lane = lax.broadcasted_iota(jnp.int32, (total, LANES), 1)
    cell_lon = lon_first + lax.broadcasted_iota(jnp.int32, (1, clon), 1).astype(jnp.float32)

    def prepare(batch):
        rows = table[batch, :total, :]
        lats[batch] = jnp.broadcast_to(rows[:, mine + 2 : mine + 3] - lat_first, (total, clon))
        dx = wrapped(cell_lon - rows[:, mine + 3 : mine + 4], 1.0 * nlon)
        gaps[batch] = dx * dx
        high, low = split(rows * (1.0 / (full - 1.0)))
        high = high.astype(jnp.float32)
        turned = pltpu.roll(low.astype(jnp.float32), full, 1)
        first = jnp.where(lane < full, high, turned)
        spill = 2 * full - LANES
        second = jnp.where(lane < spill, turned, pltpu.roll(high, spill, 1))
        priors[batch, :, :LANES] = first.astype(jnp.bfloat16)
        priors[batch, :, LANES:] = second.astype(jnp.bfloat16)[:, : 3 * full - LANES]
        for i in range(coef_t.shape[1] // LANES):
            block = table[batch, i * LANES : (i + 1) * LANES, :]
            turned = (block[:, mine : mine + 1] - block[:, mine + 1 : mine + 2] * block).T
            coef_t[:, i * LANES : (i + 1) * LANES] = turned[:full]
        high, low = split(coef_t[:, :total])
        coefs[batch, :full, :] = high
        coefs[batch, full:, :] = low
        for i in range(2 * third // LANES):
            block = table[batch, third + i * LANES : third + (i + 1) * LANES, :]
            turned = (block[:, mine : mine + 1] - block[:, mine + 1 : mine + 2] * block).T
            high, low = split(turned[:full])
            coefs_high[batch, :full, i * LANES : (i + 1) * LANES] = high
            coefs_high[batch, full:, i * LANES : (i + 1) * LANES] = low

    share(0)
    prepare(0)
    rows = table[0]
    cov = jnp.dot(rows, cross[...], precision=HIGHEST, preferred_element_type=jnp.float32) * (1.0 / (full - 1.0))
    dy = own_lat - rows[:, mine + 2 : mine + 3]
    dx = wrapped(own_lon - rows[:, mine + 3 : mine + 4], 1.0 * nlon)
    gain = cov * gaspari_sq(dx * dx + dy * dy)
    prior[...] = prior[...] + jnp.dot(coef_t[...], gain, precision=HIGHEST, preferred_element_type=jnp.float32)
    share(1)
    prepare(1)
    own.wait()

    state_flat = state.reshape(full * levels * clat, clon)

    def update(lo, hi, coef_ref, y):
        cell_lat = y.astype(jnp.float32)
        spots = [pl.ds(l * clat + y, full, stride=levels * clat) for l in range(levels)]
        value = jnp.concatenate([state_flat[spot, :] for spot in spots], axis=1)
        for batch in range(NBATCH):
            dy = lats[batch, lo:hi, :] - cell_lat
            taper = gaspari_sq(gaps[batch, lo:hi, :] + dy * dy)
            pert = value - jnp.mean(value, axis=0, keepdims=True)
            high, low = split(pert)
            stacked = jnp.concatenate([high, high, low], axis=0)
            cov = jnp.dot(priors[batch, lo:hi, :], stacked, preferred_element_type=jnp.float32)
            ghigh, glow = split(cov * jnp.concatenate([taper] * levels, axis=1))
            both = jnp.dot(coef_ref[batch, :, : hi - lo], ghigh, preferred_element_type=jnp.float32)
            rest = jnp.dot(coef_ref[batch, :full, : hi - lo], glow, preferred_element_type=jnp.float32)
            value = value + (both[:full] + (both[full:] + rest))
        for l, spot in enumerate(spots):
            state_flat[spot, :] = value[:, l * clon : (l + 1) * clon]

    kinds = []
    for p in range(pieces):
        lo = 0 if p * STEP + 1 < RAD else third
        hi = total if clat - (p * STEP + STEP - 1) < RAD else 2 * third
        if kinds and kinds[-1][2:] == (lo, hi):
            kinds[-1] = (kinds[-1][0], p + 1, lo, hi)
        else:
            kinds.append((p, p + 1, lo, hi))

    for begin, end, lo, hi in kinds:

        def one_piece(p, carry):
            for d in range(1, parts):
                inward(p, d).wait_recv()

            def one_row(i, inner):
                update(lo, hi, coefs if lo == 0 else coefs_high, p * STEP + i)
                return inner

            lax.fori_loop(0, STEP, one_row, 0)
            for d in range(1, parts):
                outward(p, d).start()
            kept(p).start()
            return carry

        lax.fori_loop(begin, end, one_piece, 0)

    def finish(p, carry):
        for d in range(1, parts):
            inward(p, d).wait_send()
        for d in range(1, parts):
            outward(p, d).wait()
        kept(p).wait()
        return carry

    lax.fori_loop(0, pieces, finish, 0)


def body(bands, parts, members, obs_row, obs_col, obs_value, obs_error, obs_weight, obs_count):
    group, levels, clat, nlon = members.shape
    full = group * parts
    clon = nlon // parts
    slots = obs_row.shape[-1]
    assert NBATCH * slots == LANES and clon == LANES and full + 4 <= LANES and LANES < 2 * full and 3 * full <= 2 * LANES
    assert bands >= 3 and parts >= 3

    valid = jnp.arange(slots)[None] < obs_count.reshape(NBATCH, 1)
    fields = [v.reshape(NBATCH, slots).astype(jnp.float32) for v in (obs_row, obs_col, obs_value, obs_error)]
    fields += [obs_weight[:, 0, 0, l] for l in range(levels)]
    fields += [valid.astype(jnp.float32), jnp.zeros((NBATCH, slots), jnp.float32)]
    info = jnp.stack(fields, axis=0).reshape(len(fields), NBATCH * slots)

    pieces = clat // STEP
    total = 9 * slots
    padded = -(-total // LANES) * LANES
    f32, bf16 = jnp.float32, jnp.bfloat16
    dma = pltpu.SemaphoreType.DMA
    near = len(AROUND)
    return pl.pallas_call(
        functools.partial(fused_kernel, bands, parts, slots),
        out_shape=jax.ShapeDtypeStruct(members.shape, f32),
        in_specs=[pl.BlockSpec(memory_space=pltpu.VMEM), pl.BlockSpec(memory_space=pl.ANY)],
        out_specs=pl.BlockSpec(memory_space=pl.ANY),
        scratch_shapes=[
            pltpu.VMEM(members.shape, f32),
            pltpu.VMEM((full, levels, clat, clon), f32),
            pltpu.VMEM((parts,) + info.shape, f32),
            pltpu.VMEM((parts, group, LANES), f32),
            pltpu.VMEM((parts, group, LANES), f32),
            pltpu.VMEM((full, LANES), f32),
            pltpu.VMEM((LANES, LANES), f32),
            pltpu.VMEM((LANES, LANES), f32),
            pltpu.VMEM((NBATCH, LANES, LANES), f32),
            pltpu.VMEM((NBATCH, padded, LANES), f32),
            pltpu.VMEM((full, padded), f32),
            pltpu.VMEM((NBATCH, total, clon), f32),
            pltpu.VMEM((NBATCH, total, clon), f32),
            pltpu.VMEM((NBATCH, total, 3 * full), bf16),
            pltpu.VMEM((NBATCH, 2 * full, total), bf16),
            pltpu.VMEM((NBATCH, 2 * full, 6 * slots), bf16),
            dma((pieces, parts)),
            dma((pieces, parts)),
            dma((pieces, parts)),
            dma((pieces, parts)),
            dma((parts,)),
            dma((parts,)),
            dma((parts,)),
            dma((parts,)),
            dma((NBATCH, near)),
            dma((NBATCH, near)),
            dma((pieces + 2,)),
        ],
        compiler_params=pltpu.CompilerParams(collective_id=0, has_side_effects=True, vmem_limit_bytes=50 << 20),
    )(info, members)


def solution(mesh):
    placed = (
        P("lon", None, "lat", None),
        P(None, "lat", "lon", None),
        P(None, "lat", "lon", None),
        P(None, "lat", "lon", None),
        P(None, "lat", "lon", None),
        P(None, "lat", "lon", None, None),
        P(None, "lat", "lon"),
    )
    return jax.shard_map(
        functools.partial(body, mesh.shape["lat"], mesh.shape["lon"]),
        mesh=mesh,
        in_specs=placed,
        out_specs=P("lon", None, "lat", None),
        check_vma=False,
    )
```

```python
import functools

import jax
import jax.numpy as jnp
from jax import lax
from jax.experimental import pallas as pl
from jax.experimental.pallas import tpu as pltpu
from jax.sharding import PartitionSpec as P

NBATCH = 2
RAD = 48
STEP = 8
ISSUE = (1, 1, 1, 1, 4)
LANES = 128
HIGHEST = lax.Precision.HIGHEST
MESH = pl.DeviceIdType.MESH
AROUND = [(da, db) for da in (-1, 0, 1) for db in (-1, 0, 1) if (da, db) != (0, 0)]


def gaspari_sq(dist_sq):
    inverse = lax.rsqrt(jnp.maximum(dist_sq, 1e-12))
    z = dist_sq * inverse * (2.0 / RAD)
    near = (((-0.25 * z + 0.5) * z + 0.625) * z - 5.0 / 3.0) * (z * z) + 1.0
    far = (
        ((((z * (1.0 / 12.0) - 0.5) * z + 0.625) * z + 5.0 / 3.0) * z - 5.0) * z
        + 4.0
        - inverse * (RAD / 3.0)
    )
    return jnp.where(z <= 1.0, near, jnp.where(z < 2.0, far, 0.0))


def split(value):
    high = value.astype(jnp.bfloat16)
    low = (value - high.astype(jnp.float32)).astype(jnp.bfloat16)
    return high, low


def wrapped(gap, nlon):
    half = 0.5 * nlon
    return jnp.where(gap >= half, gap - nlon, jnp.where(gap < -half, gap + nlon, gap))


def fused_kernel(
    bands, parts, slots, row_ref, col_ref, value_ref, error_ref, weight_ref, count_ref, members_ref, out_ref,
    small, info_ref, mem, state, info_all, pick, prior_parts, prior, cross, pack, packed, table, coef_t,
    lats, gaps, priors, coefs, coefs_high,
    in_send, in_recv, out_send, out_recv, info_send, info_recv, pick_send, pick_recv, near_send, near_recv, own_sem, small_sem,
):
    group, levels, clat, nlon = members_ref.shape
    full = group * parts
    clon = nlon // parts
    pieces = clat // STEP
    third = 3 * slots
    total = 3 * third
    mine = full
    band = lax.axis_index("lat")
    me = lax.axis_index("lon")
    lat_first = (band * clat).astype(jnp.float32)
    lon_first = (me * clon).astype(jnp.float32)

    def to(d):
        return me ^ d

    def columns(sector):
        return pl.ds(pl.multiple_of(sector * clon, clon), clon)

    def rows_of(p):
        return pl.ds(pl.multiple_of(p * STEP, STEP), STEP)

    def inward(p, d):
        return pltpu.make_async_remote_copy(
            src_ref=members_ref.at[:, :, rows_of(p), columns(to(d))],
            dst_ref=state.at[pl.ds(me * group, group), :, rows_of(p), :],
            send_sem=in_send.at[p, d],
            recv_sem=in_recv.at[p, d],
            device_id={"lon": to(d)},
            device_id_type=MESH,
        )

    def outward(p, d):
        return pltpu.make_async_remote_copy(
            src_ref=state.at[pl.ds(to(d) * group, group), :, rows_of(p), :],
            dst_ref=out_ref.at[:, :, rows_of(p), columns(me)],
            send_sem=out_send.at[p, d],
            recv_sem=out_recv.at[p, d],
            device_id={"lon": to(d)},
            device_id_type=MESH,
        )

    def kept(p):
        return pltpu.make_async_copy(
            state.at[pl.ds(me * group, group), :, rows_of(p), :],
            out_ref.at[:, :, rows_of(p), columns(me)],
            own_sem.at[p],
        )

    def informing(d):
        return pltpu.make_async_remote_copy(
            src_ref=info_ref,
            dst_ref=info_all.at[me],
            send_sem=info_send.at[d],
            recv_sem=info_recv.at[d],
            device_id={"lon": to(d)},
            device_id_type=MESH,
        )

    def picking(d):
        return pltpu.make_async_remote_copy(
            src_ref=pick.at[to(d)],
            dst_ref=prior_parts.at[me],
            send_sem=pick_send.at[d],
            recv_sem=pick_recv.at[d],
            device_id={"lon": to(d)},
            device_id_type=MESH,
        )

    def sharing(batch, i):
        da, db = AROUND[i]
        spot = (1 - da) * 3 + 1 - db
        return pltpu.make_async_remote_copy(
            src_ref=packed.at[batch, pl.ds(batch * slots, slots), :],
            dst_ref=table.at[batch, pl.ds(spot * slots, slots), :],
            send_sem=near_send.at[batch, i],
            recv_sem=near_recv.at[batch, i],
            device_id={"lat": lax.rem(band + da + bands, bands), "lon": lax.rem(me + db + parts, parts)},
            device_id_type=MESH,
        )

    fetched = []
    for i, ref in enumerate((row_ref, col_ref, value_ref, error_ref, weight_ref)):
        fetched.append(pltpu.make_async_copy(ref, small[i], small_sem.at[i]))
        fetched[-1].start()
    whole = pltpu.make_async_copy(members_ref, mem, own_sem.at[pieces])
    whole.start()
    own = pltpu.make_async_copy(
        members_ref.at[:, :, :, columns(me)], state.at[pl.ds(me * group, group)], own_sem.at[pieces + 1]
    )
    own.start()

    barrier = pltpu.get_barrier_semaphore()
    for d in range(1, parts):
        pl.semaphore_signal(barrier, inc=1, device_id={"lon": to(d)}, device_id_type=MESH)
    for da, db in AROUND:
        if da != 0:
            pl.semaphore_signal(
                barrier,
                inc=1,
                device_id={"lat": lax.rem(band + da + bands, bands), "lon": lax.rem(me + db + parts, parts)},
                device_id_type=MESH,
            )
    info_ref[...] = jnp.zeros_like(info_ref)
    for copy in fetched:
        copy.wait()
    spot = lax.broadcasted_iota(jnp.int32, (1, slots), 1)
    for batch in range(NBATCH):
        here = slice(batch * slots, (batch + 1) * slots)
        for i in range(4):
            info_ref[i : i + 1, here] = small[i][batch, 0].astype(jnp.float32)
        info_ref[4 : 4 + levels, here] = small[4][batch, 0, 0]
        info_ref[4 + levels : 5 + levels, here] = jnp.where(spot < count_ref[batch], 1.0, 0.0)
    pl.semaphore_wait(barrier, parts - 1 + 6)

    for d in range(1, parts):
        informing(d).start()

    def send_in(p, carry):
        for d in range(1, parts):
            inward(p, d).start()
        return carry

    def send_more(stage):
        first = sum(ISSUE[:stage])
        if ISSUE[stage]:
            lax.fori_loop(first, first + ISSUE[stage], send_in, 0)

    send_more(0)

    for d in range(1, parts):
        informing(d).wait()
    info_all[me] = info_ref[...]
    whole.wait()
    cell = lax.broadcasted_iota(jnp.int32, (clon, LANES), 0).astype(jnp.float32)
    grid_row = lax.broadcasted_iota(jnp.int32, (clat, LANES), 0).astype(jnp.float32)

    def pick_for(sector):
        about = info_all[sector]
        hot = jnp.where(cell == about[1:2], 1.0, 0.0).astype(jnp.bfloat16)
        chosen = grid_row == about[0:1]
        weight = jnp.stack([jnp.where(chosen, about[4 + l : 5 + l], 0.0) for l in range(levels)], axis=0)
        for k in range(group):
            values = mem[k, :, :, columns(sector)].reshape(levels * clat, clon)
            high, low = split(values)
            rest = values - high.astype(jnp.float32) - low.astype(jnp.float32)
            found = jnp.dot(
                jnp.concatenate([high, low, rest.astype(jnp.bfloat16)], axis=1),
                jnp.concatenate([hot, hot, hot], axis=0),
                preferred_element_type=jnp.float32,
            ).reshape(levels, clat, LANES)
            pick[sector, k : k + 1, :] = jnp.sum(
                jnp.sum(found * weight, axis=0), axis=0, keepdims=True
            )

    def pick_other(d, carry):
        pick_for(to(d))
        picking(d).start()
        return carry

    lax.fori_loop(1, parts, pick_other, 0)
    send_more(1)
    pick_for(me)
    prior_parts[me] = pick[me]
    for d in range(1, parts):
        picking(d).wait()
    for i in range(parts):
        prior[i * group : (i + 1) * group, :] = prior_parts[i]

    cross[...] = jnp.zeros_like(cross)
    pack[...] = jnp.zeros_like(pack)
    for batch in range(NBATCH):
        table[batch, total:, :] = jnp.zeros((table.shape[1] - total, LANES), jnp.float32)
    own_lat = lat_first + info_ref[0:1, :]
    own_lon = lon_first + info_ref[1:2, :]

    def share(batch):
        points = prior[...]
        mean = jnp.mean(points, axis=0, keepdims=True)
        pert = points - mean
        spread = jnp.sum(pert * pert, axis=0, keepdims=True) / (full - 1.0)
        err = info_ref[3:4, :]
        valid = info_ref[4 + levels : 5 + levels, :]
        denom = spread + err
        pack[:full, :] = pert
        pack[mine : mine + 1, :] = valid * (info_ref[2:3, :] - mean) / denom
        pack[mine + 1 : mine + 2, :] = valid / (denom * (1.0 + jnp.sqrt(err / denom)))
        pack[mine + 2 : mine + 3, :] = own_lat
        pack[mine + 3 : mine + 4, :] = own_lon
        if batch == 0:
            cross[:full, :] = pert
        packed[batch] = pack[...].T
        for i in range(len(AROUND)):
            sharing(batch, i).start()
        send_more(2 + batch)
        table[batch, 4 * slots : 5 * slots, :] = packed[batch, batch * slots : (batch + 1) * slots, :]
        for i in range(len(AROUND)):
            sharing(batch, i).wait()

    lane = lax.broadcasted_iota(jnp.int32, (total, LANES), 1)
    cell_lon = lon_first + lax.broadcasted_iota(jnp.int32, (1, clon), 1).astype(jnp.float32)

    def prepare(batch):
        rows = table[batch, :total, :]
        lats[batch] = jnp.broadcast_to(rows[:, mine + 2 : mine + 3] - lat_first, (total, clon))
        dx = wrapped(cell_lon - rows[:, mine + 3 : mine + 4], 1.0 * nlon)
        gaps[batch] = dx * dx
        high, low = split(rows * (1.0 / (full - 1.0)))
        high = high.astype(jnp.float32)
        turned = pltpu.roll(low.astype(jnp.float32), full, 1)
        first = jnp.where(lane < full, high, turned)
        spill = 2 * full - LANES
        second = jnp.where(lane < spill, turned, pltpu.roll(high, spill, 1))
        priors[batch, :, :LANES] = first.astype(jnp.bfloat16)
        priors[batch, :, LANES:] = second.astype(jnp.bfloat16)[:, : 3 * full - LANES]
        for i in range(coef_t.shape[1] // LANES):
            block = table[batch, i * LANES : (i + 1) * LANES, :]
            turned = (block[:, mine : mine + 1] - block[:, mine + 1 : mine + 2] * block).T
            coef_t[:, i * LANES : (i + 1) * LANES] = turned[:full]
        high, low = split(coef_t[:, :total])
        coefs[batch, :full, :] = high
        coefs[batch, full:, :] = low
        for i in range(2 * third // LANES):
            block = table[batch, third + i * LANES : third + (i + 1) * LANES, :]
            turned = (block[:, mine : mine + 1] - block[:, mine + 1 : mine + 2] * block).T
            high, low = split(turned[:full])
            coefs_high[batch, :full, i * LANES : (i + 1) * LANES] = high
            coefs_high[batch, full:, i * LANES : (i + 1) * LANES] = low

    share(0)
    prepare(0)
    rows = table[0]
    cov = jnp.dot(rows, cross[...], precision=HIGHEST, preferred_element_type=jnp.float32) * (1.0 / (full - 1.0))
    dy = own_lat - rows[:, mine + 2 : mine + 3]
    dx = wrapped(own_lon - rows[:, mine + 3 : mine + 4], 1.0 * nlon)
    gain = cov * gaspari_sq(dx * dx + dy * dy)
    prior[...] = prior[...] + jnp.dot(coef_t[...], gain, precision=HIGHEST, preferred_element_type=jnp.float32)
    share(1)
    send_more(4)
    prepare(1)
    own.wait()

    state_flat = state.reshape(full * levels * clat, clon)

    def update(lo, hi, coef_ref, y):
        cell_lat = y.astype(jnp.float32)
        spots = [pl.ds(l * clat + y, full, stride=levels * clat) for l in range(levels)]
        value = jnp.concatenate([state_flat[spot, :] for spot in spots], axis=1)
        for batch in range(NBATCH):
            dy = lats[batch, lo:hi, :] - cell_lat
            taper = gaspari_sq(gaps[batch, lo:hi, :] + dy * dy)
            pert = value - jnp.mean(value, axis=0, keepdims=True)
            high, low = split(pert)
            stacked = jnp.concatenate([high, high, low], axis=0)
            cov = jnp.dot(priors[batch, lo:hi, :], stacked, preferred_element_type=jnp.float32)
            ghigh, glow = split(cov * jnp.concatenate([taper] * levels, axis=1))
            both = jnp.dot(coef_ref[batch, :, : hi - lo], ghigh, preferred_element_type=jnp.float32)
            rest = jnp.dot(coef_ref[batch, :full, : hi - lo], glow, preferred_element_type=jnp.float32)
            value = value + (both[:full] + (both[full:] + rest))
        for l, spot in enumerate(spots):
            state_flat[spot, :] = value[:, l * clon : (l + 1) * clon]

    kinds = []
    for p in range(pieces):
        lo = 0 if p * STEP + 1 < RAD else third
        hi = total if clat - (p * STEP + STEP - 1) < RAD else 2 * third
        if kinds and kinds[-1][2:] == (lo, hi):
            kinds[-1] = (kinds[-1][0], p + 1, lo, hi)
        else:
            kinds.append((p, p + 1, lo, hi))

    for begin, end, lo, hi in kinds:

        def one_piece(p, carry):
            for d in range(1, parts):
                inward(p, d).wait_recv()

            def one_row(i, inner):
                update(lo, hi, coefs if lo == 0 else coefs_high, p * STEP + i)
                return inner

            lax.fori_loop(0, STEP, one_row, 0)
            for d in range(1, parts):
                outward(p, d).start()
            kept(p).start()
            return carry

        lax.fori_loop(begin, end, one_piece, 0)

    def finish(p, carry):
        for d in range(1, parts):
            inward(p, d).wait_send()
        for d in range(1, parts):
            outward(p, d).wait()
        kept(p).wait()
        return carry

    lax.fori_loop(0, pieces, finish, 0)


def body(bands, parts, members, obs_row, obs_col, obs_value, obs_error, obs_weight, obs_count):
    group, levels, clat, nlon = members.shape
    full = group * parts
    clon = nlon // parts
    slots = obs_row.shape[-1]
    assert NBATCH * slots == LANES and clon == LANES and full + 4 <= LANES and LANES < 2 * full and 3 * full <= 2 * LANES
    assert parts & (parts - 1) == 0 and levels <= 3 and bands >= 3 and parts >= 3

    smalls = (obs_row, obs_col, obs_value, obs_error, obs_weight)
    pieces = clat // STEP
    total = 9 * slots
    padded = -(-total // LANES) * LANES
    f32, bf16 = jnp.float32, jnp.bfloat16
    dma = pltpu.SemaphoreType.DMA
    near = len(AROUND)
    return pl.pallas_call(
        functools.partial(fused_kernel, bands, parts, slots),
        out_shape=pltpu.VMEM(members.shape, f32),
        in_specs=[pl.BlockSpec(memory_space=pl.ANY)] * len(smalls)
        + [pl.BlockSpec(memory_space=pltpu.SMEM), pl.BlockSpec(memory_space=pl.ANY)],
        out_specs=pl.BlockSpec(memory_space=pltpu.VMEM),
        scratch_shapes=[
            [pltpu.VMEM(v.shape, v.dtype) for v in smalls],
            pltpu.VMEM((8, LANES), f32),
            pltpu.VMEM(members.shape, f32),
            pltpu.VMEM((full, levels, clat, clon), f32),
            pltpu.VMEM((parts, 8, LANES), f32),
            pltpu.VMEM((parts, group, LANES), f32),
            pltpu.VMEM((parts, group, LANES), f32),
            pltpu.VMEM((full, LANES), f32),
            pltpu.VMEM((LANES, LANES), f32),
            pltpu.VMEM((LANES, LANES), f32),
            pltpu.VMEM((NBATCH, LANES, LANES), f32),
            pltpu.VMEM((NBATCH, padded, LANES), f32),
            pltpu.VMEM((full, padded), f32),
            pltpu.VMEM((NBATCH, total, clon), f32),
            pltpu.VMEM((NBATCH, total, clon), f32),
            pltpu.VMEM((NBATCH, total, 3 * full), bf16),
            pltpu.VMEM((NBATCH, 2 * full, total), bf16),
            pltpu.VMEM((NBATCH, 2 * full, 6 * slots), bf16),
            dma((pieces, parts)),
            dma((pieces, parts)),
            dma((pieces, parts)),
            dma((pieces, parts)),
            dma((parts,)),
            dma((parts,)),
            dma((parts,)),
            dma((parts,)),
            dma((NBATCH, near)),
            dma((NBATCH, near)),
            dma((pieces + 2,)),
            dma((len(smalls),)),
        ],
        compiler_params=pltpu.CompilerParams(collective_id=0, has_side_effects=True, vmem_limit_bytes=50 << 20),
    )(*smalls, obs_count.reshape(NBATCH), members)


def solution(mesh):
    placed = (
        P("lon", None, "lat", None),
        P(None, "lat", "lon", None),
        P(None, "lat", "lon", None),
        P(None, "lat", "lon", None),
        P(None, "lat", "lon", None),
        P(None, "lat", "lon", None, None),
        P(None, "lat", "lon"),
    )
    return jax.shard_map(
        functools.partial(body, mesh.shape["lat"], mesh.shape["lon"]),
        mesh=mesh,
        in_specs=placed,
        out_specs=P("lon", None, "lat", None),
        check_vma=False,
    )
```

```python
import functools

import jax
import jax.numpy as jnp
from jax import lax
from jax.experimental import pallas as pl
from jax.experimental.pallas import tpu as pltpu
from jax.sharding import PartitionSpec as P

NBATCH = 2
RAD = 48
STEP = 8
ISSUE = (1, 1, 1, 0, 1, 0, 4)
LANES = 128
HIGHEST = lax.Precision.HIGHEST
MESH = pl.DeviceIdType.MESH


def gaspari_sq(dist_sq):
    inverse = lax.rsqrt(jnp.maximum(dist_sq, 1e-12))
    z = dist_sq * inverse * (2.0 / RAD)
    near = (((-0.25 * z + 0.5) * z + 0.625) * z - 5.0 / 3.0) * (z * z) + 1.0
    far = (
        ((((z * (1.0 / 12.0) - 0.5) * z + 0.625) * z + 5.0 / 3.0) * z - 5.0) * z
        + 4.0
        - inverse * (RAD / 3.0)
    )
    return jnp.where(z <= 1.0, near, jnp.where(z < 2.0, far, 0.0))


def split(value):
    high = value.astype(jnp.bfloat16)
    low = (value - high.astype(jnp.float32)).astype(jnp.bfloat16)
    return high, low


def wrapped(gap, nlon):
    half = 0.5 * nlon
    return jnp.where(gap >= half, gap - nlon, jnp.where(gap < -half, gap + nlon, gap))


def fused_kernel(
    bands, parts, slots, row_ref, col_ref, value_ref, error_ref, weight_ref, count_ref, members_ref, out_ref,
    small, info_ref, about_ref, mem, state, info_all, pick, prior_parts, prior, cross, pack, packed, table, coef_t,
    lats, gaps, priors, coefs, coefs_high,
    in_send, in_recv, out_send, out_recv, info_send, info_recv, pick_send, pick_recv, near_send, near_recv, own_sem, small_sem,
):
    group, levels, clat, nlon = members_ref.shape
    full = group * parts
    clon = nlon // parts
    pieces = clat // STEP
    third = 3 * slots
    total = 3 * third
    mine = full
    band = lax.axis_index("lat")
    me = lax.axis_index("lon")
    lat_first = (band * clat).astype(jnp.float32)
    lon_first = (me * clon).astype(jnp.float32)

    def to(d):
        return me ^ d

    def columns(sector):
        return pl.ds(pl.multiple_of(sector * clon, clon), clon)

    def rows_of(p):
        return pl.ds(pl.multiple_of(p * STEP, STEP), STEP)

    def inward(p, d):
        return pltpu.make_async_remote_copy(
            src_ref=members_ref.at[:, :, rows_of(p), columns(to(d))],
            dst_ref=state.at[pl.ds(me * group, group), :, rows_of(p), :],
            send_sem=in_send.at[p, d],
            recv_sem=in_recv.at[p, d],
            device_id={"lon": to(d)},
            device_id_type=MESH,
        )

    def outward(p, d):
        return pltpu.make_async_remote_copy(
            src_ref=state.at[pl.ds(to(d) * group, group), :, rows_of(p), :],
            dst_ref=out_ref.at[:, :, rows_of(p), columns(me)],
            send_sem=out_send.at[p, d],
            recv_sem=out_recv.at[p, d],
            device_id={"lon": to(d)},
            device_id_type=MESH,
        )

    def kept(p):
        return pltpu.make_async_copy(
            state.at[pl.ds(me * group, group), :, rows_of(p), :],
            out_ref.at[:, :, rows_of(p), columns(me)],
            own_sem.at[p],
        )

    def informing(d):
        return pltpu.make_async_remote_copy(
            src_ref=about_ref,
            dst_ref=info_all.at[me],
            send_sem=info_send.at[d],
            recv_sem=info_recv.at[d],
            device_id={"lon": to(d)},
            device_id_type=MESH,
        )

    def picking(d):
        return pltpu.make_async_remote_copy(
            src_ref=pick.at[to(d)],
            dst_ref=prior_parts.at[me],
            send_sem=pick_send.at[d],
            recv_sem=pick_recv.at[d],
            device_id={"lon": to(d)},
            device_id_type=MESH,
        )

    def lon_share(batch, side):
        shift = 2 * side - 1
        spot = 4 - shift
        return pltpu.make_async_remote_copy(
            src_ref=packed.at[batch, pl.ds(batch * slots, slots), :],
            dst_ref=table.at[batch, pl.ds(spot * slots, slots), :],
            send_sem=near_send.at[batch, side],
            recv_sem=near_recv.at[batch, side],
            device_id={"lon": lax.rem(me + shift + parts, parts)},
            device_id_type=MESH,
        )

    def lat_share(batch, side):
        shift = 2 * side - 1
        return pltpu.make_async_remote_copy(
            src_ref=table.at[batch, pl.ds(third, third), :],
            dst_ref=table.at[batch, pl.ds((1 - shift) * third, third), :],
            send_sem=near_send.at[batch, 2 + side],
            recv_sem=near_recv.at[batch, 2 + side],
            device_id={"lat": lax.rem(band + shift + bands, bands)},
            device_id_type=MESH,
        )

    barrier = pltpu.get_barrier_semaphore()
    for d in range(1, parts):
        pl.semaphore_signal(barrier, inc=1, device_id={"lon": to(d)}, device_id_type=MESH)
    for shift in (-1, 1):
        beside = lax.rem(band + shift + bands, bands)
        pl.semaphore_signal(barrier, inc=1, device_id={"lat": beside}, device_id_type=MESH)
    fetched = []
    for i, ref in enumerate((row_ref, col_ref, value_ref, error_ref, weight_ref)):
        fetched.append(pltpu.make_async_copy(ref, small[i], small_sem.at[i]))
        fetched[-1].start()
    whole = pltpu.make_async_copy(members_ref, mem, own_sem.at[pieces])
    whole.start()
    own = pltpu.make_async_copy(
        members_ref.at[:, :, :, columns(me)], state.at[pl.ds(me * group, group)], own_sem.at[pieces + 1]
    )
    own.start()

    info_ref[...] = jnp.zeros_like(info_ref)
    for copy in fetched:
        copy.wait()
    spot = lax.broadcasted_iota(jnp.int32, (1, slots), 1)
    for batch in range(NBATCH):
        here = slice(batch * slots, (batch + 1) * slots)
        for i in range(4):
            info_ref[i : i + 1, here] = small[i][batch, 0].astype(jnp.float32)
        info_ref[4 : 4 + levels, here] = small[4][batch, 0, 0]
        info_ref[4 + levels : 5 + levels, here] = jnp.where(spot < count_ref[batch], 1.0, 0.0)
    about_ref[:2, :] = info_ref[:2, :]
    about_ref[2:, :] = info_ref[4 : 4 + levels, :]
    pl.semaphore_wait(barrier, parts - 1 + 2)

    for d in range(1, parts):
        informing(d).start()

    def send_in(p, carry):
        for d in range(1, parts):
            inward(p, d).start()
        return carry

    def send_more(stage):
        first = sum(ISSUE[:stage])
        if ISSUE[stage]:
            lax.fori_loop(first, first + ISSUE[stage], send_in, 0)

    send_more(0)

    for d in range(1, parts):
        informing(d).wait()
    info_all[me] = about_ref[...]
    whole.wait()
    cell = lax.broadcasted_iota(jnp.int32, (clon, LANES), 0).astype(jnp.float32)
    grid_row = lax.broadcasted_iota(jnp.int32, (clat, LANES), 0).astype(jnp.float32)

    def pick_for(sector):
        about = info_all[sector]
        hot = jnp.where(cell == about[1:2], 1.0, 0.0).astype(jnp.bfloat16)
        chosen = grid_row == about[0:1]
        weight = jnp.stack([jnp.where(chosen, about[2 + l : 3 + l], 0.0) for l in range(levels)], axis=0)
        for k in range(group):
            values = mem[k, :, :, columns(sector)].reshape(levels * clat, clon)
            high, low = split(values)
            rest = values - high.astype(jnp.float32) - low.astype(jnp.float32)
            found = jnp.dot(
                jnp.concatenate([high, low, rest.astype(jnp.bfloat16)], axis=1),
                jnp.concatenate([hot, hot, hot], axis=0),
                preferred_element_type=jnp.float32,
            ).reshape(levels, clat, LANES)
            pick[sector, k : k + 1, :] = jnp.sum(
                jnp.sum(found * weight, axis=0), axis=0, keepdims=True
            )

    def pick_other(d, carry):
        pick_for(to(d))
        picking(d).start()
        return carry

    lax.fori_loop(1, parts, pick_other, 0)
    send_more(1)
    pick_for(me)
    prior_parts[me] = pick[me]
    for d in range(1, parts):
        picking(d).wait()
    for i in range(parts):
        prior[i * group : (i + 1) * group, :] = prior_parts[i]

    cross[...] = jnp.zeros_like(cross)
    pack[...] = jnp.zeros_like(pack)
    for batch in range(NBATCH):
        table[batch, total:, :] = jnp.zeros((table.shape[1] - total, LANES), jnp.float32)
    own_lat = lat_first + info_ref[0:1, :]
    own_lon = lon_first + info_ref[1:2, :]

    def share(batch):
        points = prior[...]
        mean = jnp.mean(points, axis=0, keepdims=True)
        pert = points - mean
        spread = jnp.sum(pert * pert, axis=0, keepdims=True) / (full - 1.0)
        err = info_ref[3:4, :]
        valid = info_ref[4 + levels : 5 + levels, :]
        denom = spread + err
        pack[:full, :] = pert
        pack[mine : mine + 1, :] = valid * (info_ref[2:3, :] - mean) / denom
        pack[mine + 1 : mine + 2, :] = valid / (denom * (1.0 + jnp.sqrt(err / denom)))
        pack[mine + 2 : mine + 3, :] = own_lat
        pack[mine + 3 : mine + 4, :] = own_lon
        if batch == 0:
            cross[:full, :] = pert
        packed[batch] = pack[...].T
        for side in range(2):
            lon_share(batch, side).start()
        send_more(2 + 2 * batch)
        table[batch, 4 * slots : 5 * slots, :] = packed[batch, batch * slots : (batch + 1) * slots, :]
        for side in range(2):
            lon_share(batch, side).wait()
        for side in range(2):
            lat_share(batch, side).start()
        send_more(3 + 2 * batch)
        for side in range(2):
            lat_share(batch, side).wait()

    lane = lax.broadcasted_iota(jnp.int32, (total, LANES), 1)
    cell_lon = lon_first + lax.broadcasted_iota(jnp.int32, (1, clon), 1).astype(jnp.float32)

    def prepare(batch):
        rows = table[batch, :total, :]
        lats[batch] = jnp.broadcast_to(rows[:, mine + 2 : mine + 3] - lat_first, (total, clon))
        dx = wrapped(cell_lon - rows[:, mine + 3 : mine + 4], 1.0 * nlon)
        gaps[batch] = dx * dx
        high, low = split(rows * (1.0 / (full - 1.0)))
        high = high.astype(jnp.float32)
        turned = pltpu.roll(low.astype(jnp.float32), full, 1)
        first = jnp.where(lane < full, high, turned)
        spill = 2 * full - LANES
        second = jnp.where(lane < spill, turned, pltpu.roll(high, spill, 1))
        priors[batch, :, :LANES] = first.astype(jnp.bfloat16)
        priors[batch, :, LANES:] = second.astype(jnp.bfloat16)[:, : 3 * full - LANES]
        for i in range(coef_t.shape[1] // LANES):
            block = table[batch, i * LANES : (i + 1) * LANES, :]
            turned = (block[:, mine : mine + 1] - block[:, mine + 1 : mine + 2] * block).T
            coef_t[:, i * LANES : (i + 1) * LANES] = turned[:full]
        high, low = split(coef_t[:, :total])
        coefs[batch, :full, :] = high
        coefs[batch, full:, :] = low
        for i in range(2 * third // LANES):
            block = table[batch, third + i * LANES : third + (i + 1) * LANES, :]
            turned = (block[:, mine : mine + 1] - block[:, mine + 1 : mine + 2] * block).T
            high, low = split(turned[:full])
            coefs_high[batch, :full, i * LANES : (i + 1) * LANES] = high
            coefs_high[batch, full:, i * LANES : (i + 1) * LANES] = low

    share(0)
    prepare(0)
    rows = table[0]
    cov = jnp.dot(rows, cross[...], precision=HIGHEST, preferred_element_type=jnp.float32) * (1.0 / (full - 1.0))
    dy = own_lat - rows[:, mine + 2 : mine + 3]
    dx = wrapped(own_lon - rows[:, mine + 3 : mine + 4], 1.0 * nlon)
    gain = cov * gaspari_sq(dx * dx + dy * dy)
    prior[...] = prior[...] + jnp.dot(coef_t[...], gain, precision=HIGHEST, preferred_element_type=jnp.float32)
    share(1)
    send_more(6)
    prepare(1)
    own.wait()

    state_flat = state.reshape(full * levels * clat, clon)

    def update(lo, hi, coef_ref, y):
        cell_lat = y.astype(jnp.float32)
        spots = [pl.ds(l * clat + y, full, stride=levels * clat) for l in range(levels)]
        value = jnp.concatenate([state_flat[spot, :] for spot in spots], axis=1)
        for batch in range(NBATCH):
            dy = lats[batch, lo:hi, :] - cell_lat
            taper = gaspari_sq(gaps[batch, lo:hi, :] + dy * dy)
            pert = value - jnp.mean(value, axis=0, keepdims=True)
            high, low = split(pert)
            stacked = jnp.concatenate([high, high, low], axis=0)
            cov = jnp.dot(priors[batch, lo:hi, :], stacked, preferred_element_type=jnp.float32)
            ghigh, glow = split(cov * jnp.concatenate([taper] * levels, axis=1))
            both = jnp.dot(coef_ref[batch, :, : hi - lo], ghigh, preferred_element_type=jnp.float32)
            rest = jnp.dot(coef_ref[batch, :full, : hi - lo], glow, preferred_element_type=jnp.float32)
            value = value + (both[:full] + (both[full:] + rest))
        for l, spot in enumerate(spots):
            state_flat[spot, :] = value[:, l * clon : (l + 1) * clon]

    kinds = []
    for p in range(pieces):
        lo = 0 if p * STEP + 1 < RAD else third
        hi = total if clat - (p * STEP + STEP - 1) < RAD else 2 * third
        if kinds and kinds[-1][2:] == (lo, hi):
            kinds[-1] = (kinds[-1][0], p + 1, lo, hi)
        else:
            kinds.append((p, p + 1, lo, hi))

    for begin, end, lo, hi in kinds:

        def one_piece(p, carry):
            for d in range(1, parts):
                inward(p, d).wait_recv()

            def one_row(i, inner):
                update(lo, hi, coefs if lo == 0 else coefs_high, p * STEP + i)
                return inner

            lax.fori_loop(0, STEP, one_row, 0)
            for d in range(1, parts):
                outward(p, d).start()
            kept(p).start()
            return carry

        lax.fori_loop(begin, end, one_piece, 0)

    def finish(p, carry):
        for d in range(1, parts):
            inward(p, d).wait_send()
        for d in range(1, parts):
            outward(p, d).wait()
        kept(p).wait()
        return carry

    lax.fori_loop(0, pieces, finish, 0)


def body(bands, parts, members, obs_row, obs_col, obs_value, obs_error, obs_weight, obs_count):
    group, levels, clat, nlon = members.shape
    full = group * parts
    clon = nlon // parts
    slots = obs_row.shape[-1]
    assert NBATCH * slots == LANES and clon == LANES and full + 4 <= LANES and LANES < 2 * full and 3 * full <= 2 * LANES
    assert parts & (parts - 1) == 0 and levels <= 3 and bands >= 3 and parts >= 3

    smalls = (obs_row, obs_col, obs_value, obs_error, obs_weight)
    pieces = clat // STEP
    total = 9 * slots
    padded = -(-total // LANES) * LANES
    f32, bf16 = jnp.float32, jnp.bfloat16
    dma = pltpu.SemaphoreType.DMA
    return pl.pallas_call(
        functools.partial(fused_kernel, bands, parts, slots),
        out_shape=pltpu.VMEM(members.shape, f32),
        in_specs=[pl.BlockSpec(memory_space=pl.ANY)] * len(smalls)
        + [pl.BlockSpec(memory_space=pltpu.SMEM), pl.BlockSpec(memory_space=pl.ANY)],
        out_specs=pl.BlockSpec(memory_space=pltpu.VMEM),
        scratch_shapes=[
            [pltpu.VMEM(v.shape, v.dtype) for v in smalls],
            pltpu.VMEM((8, LANES), f32),
            pltpu.VMEM((2 + levels, LANES), f32),
            pltpu.VMEM(members.shape, f32),
            pltpu.VMEM((full, levels, clat, clon), f32),
            pltpu.VMEM((parts, 2 + levels, LANES), f32),
            pltpu.VMEM((parts, group, LANES), f32),
            pltpu.VMEM((parts, group, LANES), f32),
            pltpu.VMEM((full, LANES), f32),
            pltpu.VMEM((LANES, LANES), f32),
            pltpu.VMEM((LANES, LANES), f32),
            pltpu.VMEM((NBATCH, LANES, LANES), f32),
            pltpu.VMEM((NBATCH, padded, LANES), f32),
            pltpu.VMEM((full, padded), f32),
            pltpu.VMEM((NBATCH, total, clon), f32),
            pltpu.VMEM((NBATCH, total, clon), f32),
            pltpu.VMEM((NBATCH, total, 3 * full), bf16),
            pltpu.VMEM((NBATCH, 2 * full, total), bf16),
            pltpu.VMEM((NBATCH, 2 * full, 6 * slots), bf16),
            dma((pieces, parts)),
            dma((pieces, parts)),
            dma((pieces, parts)),
            dma((pieces, parts)),
            dma((parts,)),
            dma((parts,)),
            dma((parts,)),
            dma((parts,)),
            dma((NBATCH, 4)),
            dma((NBATCH, 4)),
            dma((pieces + 2,)),
            dma((len(smalls),)),
        ],
        compiler_params=pltpu.CompilerParams(collective_id=0, has_side_effects=True, vmem_limit_bytes=50 << 20),
    )(*smalls, obs_count.reshape(NBATCH), members)


def solution(mesh):
    placed = (
        P("lon", None, "lat", None),
        P(None, "lat", "lon", None),
        P(None, "lat", "lon", None),
        P(None, "lat", "lon", None),
        P(None, "lat", "lon", None),
        P(None, "lat", "lon", None, None),
        P(None, "lat", "lon"),
    )
    return jax.shard_map(
        functools.partial(body, mesh.shape["lat"], mesh.shape["lon"]),
        mesh=mesh,
        in_specs=placed,
        out_specs=P("lon", None, "lat", None),
        check_vma=False,
    )
```

```python
import functools

import jax
import jax.numpy as jnp
from jax import lax
from jax.experimental import pallas as pl
from jax.experimental.pallas import tpu as pltpu
from jax.sharding import PartitionSpec as P

NBATCH = 2
RAD = 48
STEP = 8
ISSUE = (1, 1, 1, 0, 1, 0, 4)
LANES = 128
HIGHEST = lax.Precision.HIGHEST
MESH = pl.DeviceIdType.MESH


def gaspari_sq(dist_sq):
    inverse = lax.rsqrt(jnp.maximum(dist_sq, 1e-12))
    z = dist_sq * inverse * (2.0 / RAD)
    near = (((-0.25 * z + 0.5) * z + 0.625) * z - 5.0 / 3.0) * (z * z) + 1.0
    far = (
        ((((z * (1.0 / 12.0) - 0.5) * z + 0.625) * z + 5.0 / 3.0) * z - 5.0) * z
        + 4.0
        - inverse * (RAD / 3.0)
    )
    return jnp.where(z <= 1.0, near, jnp.where(z < 2.0, far, 0.0))


def split(value):
    high = value.astype(jnp.bfloat16)
    low = (value - high.astype(jnp.float32)).astype(jnp.bfloat16)
    return high, low


def wrapped(gap, nlon):
    half = 0.5 * nlon
    return jnp.where(gap >= half, gap - nlon, jnp.where(gap < -half, gap + nlon, gap))


def fused_kernel(
    bands, parts, slots, row_ref, col_ref, value_ref, error_ref, weight_ref, count_ref, members_ref, out_ref,
    small, counts, info_ref, about_ref, mem, state, info_all, pick, prior_parts, prior, cross, pack, packed, table, coef_t,
    lats, gaps, priors, coefs, coefs_high,
    in_send, in_recv, out_send, out_recv, info_send, info_recv, pick_send, pick_recv, near_send, near_recv, own_sem, small_sem,
):
    group, levels, clat, nlon = members_ref.shape
    full = group * parts
    clon = nlon // parts
    pieces = clat // STEP
    third = 3 * slots
    total = 3 * third
    mine = full
    band = lax.axis_index("lat")
    me = lax.axis_index("lon")
    lat_first = (band * clat).astype(jnp.float32)
    lon_first = (me * clon).astype(jnp.float32)

    def to(d):
        return me ^ d

    order = [2, 3, 1, *range(4, parts)]

    def columns(sector):
        return pl.ds(pl.multiple_of(sector * clon, clon), clon)

    def rows_of(p):
        return pl.ds(pl.multiple_of(p * STEP, STEP), STEP)

    def inward(p, d):
        return pltpu.make_async_remote_copy(
            src_ref=members_ref.at[:, :, rows_of(p), columns(to(d))],
            dst_ref=state.at[pl.ds(me * group, group), :, rows_of(p), :],
            send_sem=in_send.at[p, d],
            recv_sem=in_recv.at[p, d],
            device_id={"lon": to(d)},
            device_id_type=MESH,
        )

    def outward(p, d):
        return pltpu.make_async_remote_copy(
            src_ref=state.at[pl.ds(to(d) * group, group), :, rows_of(p), :],
            dst_ref=out_ref.at[:, :, rows_of(p), columns(me)],
            send_sem=out_send.at[p, d],
            recv_sem=out_recv.at[p, d],
            device_id={"lon": to(d)},
            device_id_type=MESH,
        )

    def kept(p):
        return pltpu.make_async_copy(
            state.at[pl.ds(me * group, group), :, rows_of(p), :],
            out_ref.at[:, :, rows_of(p), columns(me)],
            own_sem.at[p],
        )

    def informing(d):
        return pltpu.make_async_remote_copy(
            src_ref=about_ref,
            dst_ref=info_all.at[me],
            send_sem=info_send.at[d],
            recv_sem=info_recv.at[d],
            device_id={"lon": to(d)},
            device_id_type=MESH,
        )

    def picking(d):
        return pltpu.make_async_remote_copy(
            src_ref=pick.at[to(d)],
            dst_ref=prior_parts.at[me],
            send_sem=pick_send.at[d],
            recv_sem=pick_recv.at[d],
            device_id={"lon": to(d)},
            device_id_type=MESH,
        )

    def lon_share(batch, side):
        shift = 2 * side - 1
        spot = 4 - shift
        return pltpu.make_async_remote_copy(
            src_ref=packed.at[batch, pl.ds(batch * slots, slots), :],
            dst_ref=table.at[batch, pl.ds(spot * slots, slots), :],
            send_sem=near_send.at[batch, side],
            recv_sem=near_recv.at[batch, side],
            device_id={"lon": lax.rem(me + shift + parts, parts)},
            device_id_type=MESH,
        )

    def lat_share(batch, side):
        shift = 2 * side - 1
        return pltpu.make_async_remote_copy(
            src_ref=table.at[batch, pl.ds(third, third), :],
            dst_ref=table.at[batch, pl.ds((1 - shift) * third, third), :],
            send_sem=near_send.at[batch, 2 + side],
            recv_sem=near_recv.at[batch, 2 + side],
            device_id={"lat": lax.rem(band + shift + bands, bands)},
            device_id_type=MESH,
        )

    barrier = pltpu.get_barrier_semaphore()
    for d in range(1, parts):
        pl.semaphore_signal(barrier, inc=1, device_id={"lon": to(d)}, device_id_type=MESH)
    for shift in (-1, 1):
        beside = lax.rem(band + shift + bands, bands)
        pl.semaphore_signal(barrier, inc=1, device_id={"lat": beside}, device_id_type=MESH)
    fetched = [pltpu.make_async_copy(count_ref, counts, small_sem.at[5])]
    fetched[0].start()
    for i, ref in enumerate((row_ref, col_ref, value_ref, error_ref, weight_ref)):
        fetched.append(pltpu.make_async_copy(ref, small[i], small_sem.at[i]))
        fetched[-1].start()
    whole = pltpu.make_async_copy(members_ref, mem, own_sem.at[pieces])
    whole.start()
    own = pltpu.make_async_copy(
        members_ref.at[:, :, :, columns(me)], state.at[pl.ds(me * group, group)], own_sem.at[pieces + 1]
    )
    own.start()

    info_ref[...] = jnp.zeros_like(info_ref)
    for copy in fetched:
        copy.wait()
    spot = lax.broadcasted_iota(jnp.int32, (1, slots), 1)
    for batch in range(NBATCH):
        here = slice(batch * slots, (batch + 1) * slots)
        for i in range(4):
            info_ref[i : i + 1, here] = small[i][batch, 0].astype(jnp.float32)
        info_ref[4 : 4 + levels, here] = small[4][batch, 0, 0]
        info_ref[4 + levels : 5 + levels, here] = jnp.where(spot < counts[batch], 1.0, 0.0)
    about_ref[:2, :] = info_ref[:2, :]
    about_ref[2:, :] = info_ref[4 : 4 + levels, :]
    pl.semaphore_wait(barrier, parts - 1 + 2)

    for d in range(1, parts):
        informing(d).start()

    def send_in(p, carry):
        for d in order:
            inward(p, d).start()
        return carry

    def send_more(stage):
        first = sum(ISSUE[:stage])
        if ISSUE[stage]:
            lax.fori_loop(first, first + ISSUE[stage], send_in, 0)

    send_more(0)

    for d in range(1, parts):
        informing(d).wait()
    info_all[me] = about_ref[...]
    whole.wait()
    cell = lax.broadcasted_iota(jnp.int32, (clon, LANES), 0).astype(jnp.float32)
    grid_row = lax.broadcasted_iota(jnp.int32, (clat, LANES), 0).astype(jnp.float32)

    def pick_for(sector):
        about = info_all[sector]
        hot = jnp.where(cell == about[1:2], 1.0, 0.0).astype(jnp.bfloat16)
        chosen = grid_row == about[0:1]
        weight = jnp.stack([jnp.where(chosen, about[2 + l : 3 + l], 0.0) for l in range(levels)], axis=0)
        for k in range(group):
            values = mem[k, :, :, columns(sector)].reshape(levels * clat, clon)
            high, low = split(values)
            rest = values - high.astype(jnp.float32) - low.astype(jnp.float32)
            found = jnp.dot(
                jnp.concatenate([high, low, rest.astype(jnp.bfloat16)], axis=1),
                jnp.concatenate([hot, hot, hot], axis=0),
                preferred_element_type=jnp.float32,
            ).reshape(levels, clat, LANES)
            pick[sector, k : k + 1, :] = jnp.sum(
                jnp.sum(found * weight, axis=0), axis=0, keepdims=True
            )

    def pick_other(d, carry):
        pick_for(to(d))
        picking(d).start()
        return carry

    lax.fori_loop(1, parts, pick_other, 0)
    send_more(1)
    pick_for(me)
    prior_parts[me] = pick[me]
    for d in range(1, parts):
        picking(d).wait()
    for i in range(parts):
        prior[i * group : (i + 1) * group, :] = prior_parts[i]

    cross[...] = jnp.zeros_like(cross)
    pack[...] = jnp.zeros_like(pack)
    for batch in range(NBATCH):
        table[batch, total:, :] = jnp.zeros((table.shape[1] - total, LANES), jnp.float32)
    own_lat = lat_first + info_ref[0:1, :]
    own_lon = lon_first + info_ref[1:2, :]

    def share(batch):
        points = prior[...]
        mean = jnp.mean(points, axis=0, keepdims=True)
        pert = points - mean
        spread = jnp.sum(pert * pert, axis=0, keepdims=True) / (full - 1.0)
        err = info_ref[3:4, :]
        valid = info_ref[4 + levels : 5 + levels, :]
        denom = spread + err
        pack[:full, :] = pert
        pack[mine : mine + 1, :] = valid * (info_ref[2:3, :] - mean) / denom
        pack[mine + 1 : mine + 2, :] = valid / (denom * (1.0 + jnp.sqrt(err / denom)))
        pack[mine + 2 : mine + 3, :] = own_lat
        pack[mine + 3 : mine + 4, :] = own_lon
        if batch == 0:
            cross[:full, :] = pert
        packed[batch] = pack[...].T
        for side in range(2):
            lon_share(batch, side).start()
        send_more(2 + 2 * batch)
        table[batch, 4 * slots : 5 * slots, :] = packed[batch, batch * slots : (batch + 1) * slots, :]
        for side in range(2):
            lon_share(batch, side).wait()
        for side in range(2):
            lat_share(batch, side).start()
        send_more(3 + 2 * batch)
        for side in range(2):
            lat_share(batch, side).wait()

    lane = lax.broadcasted_iota(jnp.int32, (total, LANES), 1)
    cell_lon = lon_first + lax.broadcasted_iota(jnp.int32, (1, clon), 1).astype(jnp.float32)

    def prepare(batch):
        rows = table[batch, :total, :]
        lats[batch] = jnp.broadcast_to(rows[:, mine + 2 : mine + 3] - lat_first, (total, clon))
        dx = wrapped(cell_lon - rows[:, mine + 3 : mine + 4], 1.0 * nlon)
        gaps[batch] = dx * dx
        high, low = split(rows * (1.0 / (full - 1.0)))
        high = high.astype(jnp.float32)
        turned = pltpu.roll(low.astype(jnp.float32), full, 1)
        first = jnp.where(lane < full, high, turned)
        spill = 2 * full - LANES
        second = jnp.where(lane < spill, turned, pltpu.roll(high, spill, 1))
        priors[batch, :, :LANES] = first.astype(jnp.bfloat16)
        priors[batch, :, LANES:] = second.astype(jnp.bfloat16)[:, : 3 * full - LANES]
        for i in range(coef_t.shape[1] // LANES):
            block = table[batch, i * LANES : (i + 1) * LANES, :]
            turned = (block[:, mine : mine + 1] - block[:, mine + 1 : mine + 2] * block).T
            coef_t[:, i * LANES : (i + 1) * LANES] = turned[:full]
        high, low = split(coef_t[:, :total])
        coefs[batch, :full, :] = high
        coefs[batch, full:, :] = low
        for i in range(2 * third // LANES):
            block = table[batch, third + i * LANES : third + (i + 1) * LANES, :]
            turned = (block[:, mine : mine + 1] - block[:, mine + 1 : mine + 2] * block).T
            high, low = split(turned[:full])
            coefs_high[batch, :full, i * LANES : (i + 1) * LANES] = high
            coefs_high[batch, full:, i * LANES : (i + 1) * LANES] = low

    share(0)
    prepare(0)
    rows = table[0]
    cov = jnp.dot(rows, cross[...], precision=HIGHEST, preferred_element_type=jnp.float32) * (1.0 / (full - 1.0))
    dy = own_lat - rows[:, mine + 2 : mine + 3]
    dx = wrapped(own_lon - rows[:, mine + 3 : mine + 4], 1.0 * nlon)
    gain = cov * gaspari_sq(dx * dx + dy * dy)
    prior[...] = prior[...] + jnp.dot(coef_t[...], gain, precision=HIGHEST, preferred_element_type=jnp.float32)
    share(1)
    send_more(6)
    prepare(1)
    own.wait()

    state_flat = state.reshape(full * levels * clat, clon)

    def update(lo, hi, coef_ref, y):
        cell_lat = y.astype(jnp.float32)
        spots = [pl.ds(l * clat + y, full, stride=levels * clat) for l in range(levels)]
        value = jnp.concatenate([state_flat[spot, :] for spot in spots], axis=1)
        for batch in range(NBATCH):
            dy = lats[batch, lo:hi, :] - cell_lat
            taper = gaspari_sq(gaps[batch, lo:hi, :] + dy * dy)
            pert = value - jnp.mean(value, axis=0, keepdims=True)
            high, low = split(pert)
            stacked = jnp.concatenate([high, high, low], axis=0)
            cov = jnp.dot(priors[batch, lo:hi, :], stacked, preferred_element_type=jnp.float32)
            ghigh, glow = split(cov * jnp.concatenate([taper] * levels, axis=1))
            both = jnp.dot(coef_ref[batch, :, : hi - lo], ghigh, preferred_element_type=jnp.float32)
            rest = jnp.dot(coef_ref[batch, :full, : hi - lo], glow, preferred_element_type=jnp.float32)
            value = value + (both[:full] + (both[full:] + rest))
        for l, spot in enumerate(spots):
            state_flat[spot, :] = value[:, l * clon : (l + 1) * clon]

    kinds = []
    for p in range(pieces):
        lo = 0 if p * STEP + 1 < RAD else third
        hi = total if clat - (p * STEP + STEP - 1) < RAD else 2 * third
        if kinds and kinds[-1][2:] == (lo, hi):
            kinds[-1] = (kinds[-1][0], p + 1, lo, hi)
        else:
            kinds.append((p, p + 1, lo, hi))

    for begin, end, lo, hi in kinds:

        def one_piece(p, carry):
            for d in range(1, parts):
                inward(p, d).wait_recv()

            def one_row(i, inner):
                update(lo, hi, coefs if lo == 0 else coefs_high, p * STEP + i)
                return inner

            lax.fori_loop(0, STEP, one_row, 0)
            for d in order:
                outward(p, d).start()
            kept(p).start()
            return carry

        lax.fori_loop(begin, end, one_piece, 0)

    def finish(p, carry):
        for d in range(1, parts):
            inward(p, d).wait_send()
        for d in range(1, parts):
            outward(p, d).wait()
        kept(p).wait()
        return carry

    lax.fori_loop(0, pieces, finish, 0)


def body(bands, parts, members, obs_row, obs_col, obs_value, obs_error, obs_weight, obs_count):
    group, levels, clat, nlon = members.shape
    full = group * parts
    clon = nlon // parts
    slots = obs_row.shape[-1]
    assert NBATCH * slots == LANES and clon == LANES and full + 4 <= LANES and LANES < 2 * full and 3 * full <= 2 * LANES
    assert parts & (parts - 1) == 0 and levels <= 3 and bands >= 3 and parts >= 4

    smalls = (obs_row, obs_col, obs_value, obs_error, obs_weight)
    pieces = clat // STEP
    total = 9 * slots
    padded = -(-total // LANES) * LANES
    f32, bf16 = jnp.float32, jnp.bfloat16
    dma = pltpu.SemaphoreType.DMA
    return pl.pallas_call(
        functools.partial(fused_kernel, bands, parts, slots),
        out_shape=pltpu.VMEM(members.shape, f32),
        in_specs=[pl.BlockSpec(memory_space=pl.ANY)] * (len(smalls) + 2),
        out_specs=pl.BlockSpec(memory_space=pltpu.VMEM),
        scratch_shapes=[
            [pltpu.VMEM(v.shape, v.dtype) for v in smalls],
            pltpu.SMEM((NBATCH,), jnp.int32),
            pltpu.VMEM((8, LANES), f32),
            pltpu.VMEM((2 + levels, LANES), f32),
            pltpu.VMEM(members.shape, f32),
            pltpu.VMEM((full, levels, clat, clon), f32),
            pltpu.VMEM((parts, 2 + levels, LANES), f32),
            pltpu.VMEM((parts, group, LANES), f32),
            pltpu.VMEM((parts, group, LANES), f32),
            pltpu.VMEM((full, LANES), f32),
            pltpu.VMEM((LANES, LANES), f32),
            pltpu.VMEM((LANES, LANES), f32),
            pltpu.VMEM((NBATCH, LANES, LANES), f32),
            pltpu.VMEM((NBATCH, padded, LANES), f32),
            pltpu.VMEM((full, padded), f32),
            pltpu.VMEM((NBATCH, total, clon), f32),
            pltpu.VMEM((NBATCH, total, clon), f32),
            pltpu.VMEM((NBATCH, total, 3 * full), bf16),
            pltpu.VMEM((NBATCH, 2 * full, total), bf16),
            pltpu.VMEM((NBATCH, 2 * full, 6 * slots), bf16),
            dma((pieces, parts)),
            dma((pieces, parts)),
            dma((pieces, parts)),
            dma((pieces, parts)),
            dma((parts,)),
            dma((parts,)),
            dma((parts,)),
            dma((parts,)),
            dma((NBATCH, 4)),
            dma((NBATCH, 4)),
            dma((pieces + 2,)),
            dma((len(smalls) + 1,)),
        ],
        compiler_params=pltpu.CompilerParams(collective_id=0, has_side_effects=True, vmem_limit_bytes=50 << 20),
    )(*smalls, obs_count.reshape(NBATCH), members)


def solution(mesh):
    placed = (
        P("lon", None, "lat", None),
        P(None, "lat", "lon", None),
        P(None, "lat", "lon", None),
        P(None, "lat", "lon", None),
        P(None, "lat", "lon", None),
        P(None, "lat", "lon", None, None),
        P(None, "lat", "lon"),
    )
    return jax.shard_map(
        functools.partial(body, mesh.shape["lat"], mesh.shape["lon"]),
        mesh=mesh,
        in_specs=placed,
        out_specs=P("lon", None, "lat", None),
        check_vma=False,
    )
```

```python
import functools

import jax
import jax.numpy as jnp
from jax import lax
from jax.experimental import pallas as pl
from jax.experimental.pallas import tpu as pltpu
from jax.sharding import PartitionSpec as P

NBATCH = 2
RAD = 48
STEP = 8
ISSUE = (2, 2, 1, 1, 1, 1, 8)
LANES = 128
HIGHEST = lax.Precision.HIGHEST
MESH = pl.DeviceIdType.MESH


def gaspari_sq(dist_sq):
    inverse = lax.rsqrt(jnp.maximum(dist_sq, 1e-12))
    z = dist_sq * inverse * (2.0 / RAD)
    near = (((-0.25 * z + 0.5) * z + 0.625) * z - 5.0 / 3.0) * (z * z) + 1.0
    far = (
        ((((z * (1.0 / 12.0) - 0.5) * z + 0.625) * z + 5.0 / 3.0) * z - 5.0) * z
        + 4.0
        - inverse * (RAD / 3.0)
    )
    return jnp.where(z <= 1.0, near, jnp.where(z < 2.0, far, 0.0))


def split(value):
    high = value.astype(jnp.bfloat16)
    low = (value - high.astype(jnp.float32)).astype(jnp.bfloat16)
    return high, low


def wrapped(gap, nlon):
    half = 0.5 * nlon
    return jnp.where(gap >= half, gap - nlon, jnp.where(gap < -half, gap + nlon, gap))


def fused_kernel(
    bands, parts, slots, row_ref, col_ref, value_ref, error_ref, weight_ref, count_ref, members_ref, out_ref,
    small, counts, info_ref, about_ref, mem, state, info_all, pick, prior_parts, prior, cross, pack, opened, folded, landed, table, coef_t,
    lats, gaps, priors, coefs, coefs_high,
    in_send, in_recv, out_send, out_recv, info_send, info_recv, pick_send, pick_recv, near_send, near_recv, own_sem, small_sem,
):
    group, levels, clat, nlon = members_ref.shape
    full = group * parts
    clon = nlon // parts
    pieces = clat // STEP
    third = 3 * slots
    total = 3 * third
    mine = full
    band = lax.axis_index("lat")
    me = lax.axis_index("lon")
    lat_first = (band * clat).astype(jnp.float32)
    lon_first = (me * clon).astype(jnp.float32)

    def to(d):
        return me ^ d

    order = [2, 3, 1, *range(4, parts)]

    halves = order[: 3 + (parts - 4) // 2], order[3 + (parts - 4) // 2 :]

    def columns(sector):
        return pl.ds(pl.multiple_of(sector * clon, clon), clon)

    def rows_of(p):
        return pl.ds(pl.multiple_of(p * STEP, STEP), STEP)

    def inward(p, d):
        return pltpu.make_async_remote_copy(
            src_ref=members_ref.at[:, :, rows_of(p), columns(to(d))],
            dst_ref=state.at[pl.ds(me * group, group), :, rows_of(p), :],
            send_sem=in_send.at[p, d],
            recv_sem=in_recv.at[p, d],
            device_id={"lon": to(d)},
            device_id_type=MESH,
        )

    def outward(p, d):
        return pltpu.make_async_remote_copy(
            src_ref=state.at[pl.ds(to(d) * group, group), :, rows_of(p), :],
            dst_ref=out_ref.at[:, :, rows_of(p), columns(me)],
            send_sem=out_send.at[p, d],
            recv_sem=out_recv.at[p, d],
            device_id={"lon": to(d)},
            device_id_type=MESH,
        )

    def kept(p):
        return pltpu.make_async_copy(
            state.at[pl.ds(me * group, group), :, rows_of(p), :],
            out_ref.at[:, :, rows_of(p), columns(me)],
            own_sem.at[p],
        )

    def informing(d):
        return pltpu.make_async_remote_copy(
            src_ref=about_ref,
            dst_ref=info_all.at[me],
            send_sem=info_send.at[d],
            recv_sem=info_recv.at[d],
            device_id={"lon": to(d)},
            device_id_type=MESH,
        )

    def picking(d):
        return pltpu.make_async_remote_copy(
            src_ref=pick.at[to(d)],
            dst_ref=prior_parts.at[me],
            send_sem=pick_send.at[d],
            recv_sem=pick_recv.at[d],
            device_id={"lon": to(d)},
            device_id_type=MESH,
        )

    def lon_share(batch, side):
        shift = 2 * side - 1
        return pltpu.make_async_remote_copy(
            src_ref=folded.at[batch],
            dst_ref=landed.at[batch, side],
            send_sem=near_send.at[batch, side],
            recv_sem=near_recv.at[batch, side],
            device_id={"lon": lax.rem(me + shift + parts, parts)},
            device_id_type=MESH,
        )

    def lat_share(batch, side):
        shift = 2 * side - 1
        return pltpu.make_async_remote_copy(
            src_ref=table.at[batch, pl.ds(third, third), :],
            dst_ref=table.at[batch, pl.ds((1 - shift) * third, third), :],
            send_sem=near_send.at[batch, 2 + side],
            recv_sem=near_recv.at[batch, 2 + side],
            device_id={"lat": lax.rem(band + shift + bands, bands)},
            device_id_type=MESH,
        )

    barrier = pltpu.get_barrier_semaphore()
    for d in range(1, parts):
        pl.semaphore_signal(barrier, inc=1, device_id={"lon": to(d)}, device_id_type=MESH)
    for shift in (-1, 1):
        beside = lax.rem(band + shift + bands, bands)
        pl.semaphore_signal(barrier, inc=1, device_id={"lat": beside}, device_id_type=MESH)
    fetched = [pltpu.make_async_copy(count_ref, counts, small_sem.at[5])]
    fetched[0].start()
    for i, ref in enumerate((row_ref, col_ref, value_ref, error_ref, weight_ref)):
        fetched.append(pltpu.make_async_copy(ref, small[i], small_sem.at[i]))
        fetched[-1].start()
    whole = pltpu.make_async_copy(members_ref, mem, own_sem.at[pieces])
    whole.start()
    own = pltpu.make_async_copy(
        members_ref.at[:, :, :, columns(me)], state.at[pl.ds(me * group, group)], own_sem.at[pieces + 1]
    )
    own.start()

    info_ref[...] = jnp.zeros_like(info_ref)
    for copy in fetched:
        copy.wait()
    spot = lax.broadcasted_iota(jnp.int32, (1, slots), 1)
    for batch in range(NBATCH):
        here = slice(batch * slots, (batch + 1) * slots)
        for i in range(4):
            info_ref[i : i + 1, here] = small[i][batch, 0].astype(jnp.float32)
        info_ref[4 : 4 + levels, here] = small[4][batch, 0, 0]
        info_ref[4 + levels : 5 + levels, here] = jnp.where(spot < counts[batch], 1.0, 0.0)
    about_ref[:2, :] = info_ref[:2, :]
    about_ref[2:, :] = info_ref[4 : 4 + levels, :]
    pl.semaphore_wait(barrier, parts - 1 + 2)

    for d in range(1, parts):
        informing(d).start()

    def send_in(unit):
        for d in halves[unit % 2]:
            inward(unit // 2, d).start()

    def send_more(stage):
        first = sum(ISSUE[:stage])
        for unit in range(first, min(first + ISSUE[stage], 2 * pieces)):
            send_in(unit)

    send_more(0)

    for d in range(1, parts):
        informing(d).wait()
    info_all[me] = about_ref[...]
    whole.wait()
    cell = lax.broadcasted_iota(jnp.int32, (clon, LANES), 0).astype(jnp.float32)
    grid_row = lax.broadcasted_iota(jnp.int32, (clat, LANES), 0).astype(jnp.float32)

    def pick_for(sector):
        about = info_all[sector]
        hot = jnp.where(cell == about[1:2], 1.0, 0.0).astype(jnp.bfloat16)
        chosen = grid_row == about[0:1]
        weight = jnp.stack([jnp.where(chosen, about[2 + l : 3 + l], 0.0) for l in range(levels)], axis=0)
        for k in range(group):
            values = mem[k, :, :, columns(sector)].reshape(levels * clat, clon)
            high, low = split(values)
            rest = values - high.astype(jnp.float32) - low.astype(jnp.float32)
            found = jnp.dot(
                jnp.concatenate([high, low, rest.astype(jnp.bfloat16)], axis=1),
                jnp.concatenate([hot, hot, hot], axis=0),
                preferred_element_type=jnp.float32,
            ).reshape(levels, clat, LANES)
            pick[sector, k : k + 1, :] = jnp.sum(
                jnp.sum(found * weight, axis=0), axis=0, keepdims=True
            )

    def pick_other(d, carry):
        pick_for(to(d))
        picking(d).start()
        return carry

    lax.fori_loop(1, parts, pick_other, 0)
    send_more(1)
    pick_for(me)
    prior_parts[me] = pick[me]
    for d in range(1, parts):
        picking(d).wait()
    for i in range(parts):
        prior[i * group : (i + 1) * group, :] = prior_parts[i]

    cross[...] = jnp.zeros_like(cross)
    pack[...] = jnp.zeros_like(pack)
    opened[...] = jnp.zeros_like(opened)
    for batch in range(NBATCH):
        table[batch, total:, :] = jnp.zeros((table.shape[1] - total, LANES), jnp.float32)
    own_lat = lat_first + info_ref[0:1, :]
    own_lon = lon_first + info_ref[1:2, :]

    def share(batch):
        points = prior[...]
        mean = jnp.mean(points, axis=0, keepdims=True)
        pert = points - mean
        spread = jnp.sum(pert * pert, axis=0, keepdims=True) / (full - 1.0)
        err = info_ref[3:4, :]
        valid = info_ref[4 + levels : 5 + levels, :]
        denom = spread + err
        pack[:full, :] = pert
        pack[mine : mine + 1, :] = valid * (info_ref[2:3, :] - mean) / denom
        pack[mine + 1 : mine + 2, :] = valid / (denom * (1.0 + jnp.sqrt(err / denom)))
        pack[mine + 2 : mine + 3, :] = own_lat
        pack[mine + 3 : mine + 4, :] = own_lon
        if batch == 0:
            cross[:full, :] = pert
        fold = folded.shape[1]
        upper, lower = pack[:fold, :], pack[fold : 2 * fold, :]
        if batch == 0:
            lower = pltpu.roll(lower, slots, 1)
        else:
            upper = pltpu.roll(upper, slots, 1)
        folded[batch] = jnp.where(lax.broadcasted_iota(jnp.int32, upper.shape, 1) < slots, upper, lower)
        for side in range(2):
            lon_share(batch, side).start()
        send_more(2 + 2 * batch)
        turned = pack[...].T
        table[batch, 4 * slots : 5 * slots, :] = turned[batch * slots : (batch + 1) * slots]
        for side in range(2):
            lon_share(batch, side).wait()
            opened[:fold, :] = landed[batch, side]
            opened[fold : 2 * fold, :] = pltpu.roll(landed[batch, side], slots, 1)
            spot = 5 - 2 * side
            table[batch, spot * slots : (spot + 1) * slots, :] = opened[...].T[:slots]
        for side in range(2):
            lat_share(batch, side).start()
        send_more(3 + 2 * batch)
        for side in range(2):
            lat_share(batch, side).wait()

    lane = lax.broadcasted_iota(jnp.int32, (total, LANES), 1)
    cell_lon = lon_first + lax.broadcasted_iota(jnp.int32, (1, clon), 1).astype(jnp.float32)

    def prepare(batch):
        rows = table[batch, :total, :]
        lats[batch] = jnp.broadcast_to(rows[:, mine + 2 : mine + 3] - lat_first, (total, clon))
        dx = wrapped(cell_lon - rows[:, mine + 3 : mine + 4], 1.0 * nlon)
        gaps[batch] = dx * dx
        high, low = split(rows * (1.0 / (full - 1.0)))
        high = high.astype(jnp.float32)
        turned = pltpu.roll(low.astype(jnp.float32), full, 1)
        first = jnp.where(lane < full, high, turned)
        spill = 2 * full - LANES
        second = jnp.where(lane < spill, turned, pltpu.roll(high, spill, 1))
        priors[batch, :, :LANES] = first.astype(jnp.bfloat16)
        priors[batch, :, LANES:] = second.astype(jnp.bfloat16)[:, : 3 * full - LANES]
        for i in range(coef_t.shape[1] // LANES):
            block = table[batch, i * LANES : (i + 1) * LANES, :]
            turned = (block[:, mine : mine + 1] - block[:, mine + 1 : mine + 2] * block).T
            coef_t[:, i * LANES : (i + 1) * LANES] = turned[:full]
        high, low = split(coef_t[:, :total])
        coefs[batch, :full, :] = high
        coefs[batch, full:, :] = low
        for i in range(2 * third // LANES):
            block = table[batch, third + i * LANES : third + (i + 1) * LANES, :]
            turned = (block[:, mine : mine + 1] - block[:, mine + 1 : mine + 2] * block).T
            high, low = split(turned[:full])
            coefs_high[batch, :full, i * LANES : (i + 1) * LANES] = high
            coefs_high[batch, full:, i * LANES : (i + 1) * LANES] = low

    share(0)
    prepare(0)
    rows = table[0]
    cov = jnp.dot(rows, cross[...], precision=HIGHEST, preferred_element_type=jnp.float32) * (1.0 / (full - 1.0))
    dy = own_lat - rows[:, mine + 2 : mine + 3]
    dx = wrapped(own_lon - rows[:, mine + 3 : mine + 4], 1.0 * nlon)
    gain = cov * gaspari_sq(dx * dx + dy * dy)
    prior[...] = prior[...] + jnp.dot(coef_t[...], gain, precision=HIGHEST, preferred_element_type=jnp.float32)
    share(1)
    send_more(6)
    prepare(1)
    own.wait()

    state_flat = state.reshape(full * levels * clat, clon)

    def update(lo, hi, coef_ref, y):
        cell_lat = y.astype(jnp.float32)
        spots = [pl.ds(l * clat + y, full, stride=levels * clat) for l in range(levels)]
        value = jnp.concatenate([state_flat[spot, :] for spot in spots], axis=1)
        for batch in range(NBATCH):
            dy = lats[batch, lo:hi, :] - cell_lat
            taper = gaspari_sq(gaps[batch, lo:hi, :] + dy * dy)
            pert = value - jnp.mean(value, axis=0, keepdims=True)
            high, low = split(pert)
            stacked = jnp.concatenate([high, high, low], axis=0)
            cov = jnp.dot(priors[batch, lo:hi, :], stacked, preferred_element_type=jnp.float32)
            ghigh, glow = split(cov * jnp.concatenate([taper] * levels, axis=1))
            both = jnp.dot(coef_ref[batch, :, : hi - lo], ghigh, preferred_element_type=jnp.float32)
            rest = jnp.dot(coef_ref[batch, :full, : hi - lo], glow, preferred_element_type=jnp.float32)
            value = value + (both[:full] + (both[full:] + rest))
        for l, spot in enumerate(spots):
            state_flat[spot, :] = value[:, l * clon : (l + 1) * clon]

    kinds = []
    for p in range(pieces):
        lo = 0 if p * STEP + 1 < RAD else third
        hi = total if clat - (p * STEP + STEP - 1) < RAD else 2 * third
        if kinds and kinds[-1][2:] == (lo, hi):
            kinds[-1] = (kinds[-1][0], p + 1, lo, hi)
        else:
            kinds.append((p, p + 1, lo, hi))

    for begin, end, lo, hi in kinds:

        def one_piece(p, carry):
            for d in range(1, parts):
                inward(p, d).wait_recv()

            def one_row(i, inner):
                update(lo, hi, coefs if lo == 0 else coefs_high, p * STEP + i)
                return inner

            lax.fori_loop(0, STEP, one_row, 0)
            for d in order:
                outward(p, d).start()
            kept(p).start()
            return carry

        lax.fori_loop(begin, end, one_piece, 0)

    def finish(p, carry):
        for d in range(1, parts):
            inward(p, d).wait_send()
        for d in range(1, parts):
            outward(p, d).wait()
        kept(p).wait()
        return carry

    lax.fori_loop(0, pieces, finish, 0)


def body(bands, parts, members, obs_row, obs_col, obs_value, obs_error, obs_weight, obs_count):
    group, levels, clat, nlon = members.shape
    full = group * parts
    clon = nlon // parts
    slots = obs_row.shape[-1]
    assert NBATCH * slots == LANES and clon == LANES and full + 4 <= LANES and LANES < 2 * full and 3 * full <= 2 * LANES
    assert parts & (parts - 1) == 0 and levels <= 3 and bands >= 3 and parts >= 4

    smalls = (obs_row, obs_col, obs_value, obs_error, obs_weight)
    fold = -(-(full + 4) // 16) * 8
    pieces = clat // STEP
    total = 9 * slots
    padded = -(-total // LANES) * LANES
    f32, bf16 = jnp.float32, jnp.bfloat16
    dma = pltpu.SemaphoreType.DMA
    return pl.pallas_call(
        functools.partial(fused_kernel, bands, parts, slots),
        out_shape=pltpu.VMEM(members.shape, f32),
        in_specs=[pl.BlockSpec(memory_space=pl.ANY)] * (len(smalls) + 2),
        out_specs=pl.BlockSpec(memory_space=pltpu.VMEM),
        scratch_shapes=[
            [pltpu.VMEM(v.shape, v.dtype) for v in smalls],
            pltpu.SMEM((NBATCH,), jnp.int32),
            pltpu.VMEM((8, LANES), f32),
            pltpu.VMEM((2 + levels, LANES), f32),
            pltpu.VMEM(members.shape, f32),
            pltpu.VMEM((full, levels, clat, clon), f32),
            pltpu.VMEM((parts, 2 + levels, LANES), f32),
            pltpu.VMEM((parts, group, LANES), f32),
            pltpu.VMEM((parts, group, LANES), f32),
            pltpu.VMEM((full, LANES), f32),
            pltpu.VMEM((LANES, LANES), f32),
            pltpu.VMEM((LANES, LANES), f32),
            pltpu.VMEM((LANES, LANES), f32),
            pltpu.VMEM((NBATCH, fold, LANES), f32),
            pltpu.VMEM((NBATCH, 2, fold, LANES), f32),
            pltpu.VMEM((NBATCH, padded, LANES), f32),
            pltpu.VMEM((full, padded), f32),
            pltpu.VMEM((NBATCH, total, clon), f32),
            pltpu.VMEM((NBATCH, total, clon), f32),
            pltpu.VMEM((NBATCH, total, 3 * full), bf16),
            pltpu.VMEM((NBATCH, 2 * full, total), bf16),
            pltpu.VMEM((NBATCH, 2 * full, 6 * slots), bf16),
            dma((pieces, parts)),
            dma((pieces, parts)),
            dma((pieces, parts)),
            dma((pieces, parts)),
            dma((parts,)),
            dma((parts,)),
            dma((parts,)),
            dma((parts,)),
            dma((NBATCH, 4)),
            dma((NBATCH, 4)),
            dma((pieces + 2,)),
            dma((len(smalls) + 1,)),
        ],
        compiler_params=pltpu.CompilerParams(collective_id=0, has_side_effects=True, vmem_limit_bytes=50 << 20),
    )(*smalls, obs_count.reshape(NBATCH), members)


def solution(mesh):
    placed = (
        P("lon", None, "lat", None),
        P(None, "lat", "lon", None),
        P(None, "lat", "lon", None),
        P(None, "lat", "lon", None),
        P(None, "lat", "lon", None),
        P(None, "lat", "lon", None, None),
        P(None, "lat", "lon"),
    )
    return jax.shard_map(
        functools.partial(body, mesh.shape["lat"], mesh.shape["lon"]),
        mesh=mesh,
        in_specs=placed,
        out_specs=P("lon", None, "lat", None),
        check_vma=False,
    )
```

```python
import functools

import jax
import jax.numpy as jnp
from jax import lax
from jax.experimental import pallas as pl
from jax.experimental.pallas import tpu as pltpu
from jax.sharding import PartitionSpec as P

NBATCH = 2
RAD = 48
STEP = 8
ISSUE = (2, 2, 1, 1, 1, 1, 8)
LANES = 128
HIGHEST = lax.Precision.HIGHEST
MESH = pl.DeviceIdType.MESH


def gaspari_sq(dist_sq):
    inverse = lax.rsqrt(jnp.maximum(dist_sq, 1e-12))
    z = dist_sq * inverse * (2.0 / RAD)
    near = (((-0.25 * z + 0.5) * z + 0.625) * z - 5.0 / 3.0) * (z * z) + 1.0
    far = (
        ((((z * (1.0 / 12.0) - 0.5) * z + 0.625) * z + 5.0 / 3.0) * z - 5.0) * z
        + 4.0
        - inverse * (RAD / 3.0)
    )
    return jnp.where(z <= 1.0, near, jnp.where(z < 2.0, far, 0.0))


def split(value):
    high = value.astype(jnp.bfloat16)
    low = (value - high.astype(jnp.float32)).astype(jnp.bfloat16)
    return high, low


def wrapped(gap, nlon):
    half = 0.5 * nlon
    return jnp.where(gap >= half, gap - nlon, jnp.where(gap < -half, gap + nlon, gap))


def fused_kernel(
    bands, parts, slots, row_ref, col_ref, value_ref, error_ref, weight_ref, count_ref, members_ref, out_ref,
    small, counts, info_ref, about_ref, mem, state, info_all, pick, prior_parts, prior, cross, pack, opened, folded, landed, table, coef_t,
    lats, gaps, priors, coefs, coefs_high,
    in_send, in_recv, out_send, out_recv, info_send, info_recv, pick_send, pick_recv, near_send, near_recv, own_sem, small_sem,
):
    group, levels, clat, nlon = members_ref.shape
    full = group * parts
    clon = nlon // parts
    pieces = clat // STEP
    third = 3 * slots
    total = 3 * third
    mine = full
    band = lax.axis_index("lat")
    me = lax.axis_index("lon")
    lat_first = (band * clat).astype(jnp.float32)
    lon_first = (me * clon).astype(jnp.float32)

    def to(d):
        return me ^ d

    order = [2, 3, 1, *range(4, parts)]

    halves = order[: 3 + (parts - 4) // 2], order[3 + (parts - 4) // 2 :]

    def columns(sector):
        return pl.ds(pl.multiple_of(sector * clon, clon), clon)

    def rows_of(p):
        return pl.ds(pl.multiple_of(p * STEP, STEP), STEP)

    def inward(p, d):
        return pltpu.make_async_remote_copy(
            src_ref=members_ref.at[:, :, rows_of(p), columns(to(d))],
            dst_ref=state.at[pl.ds(me * group, group), :, rows_of(p), :],
            send_sem=in_send.at[p, d],
            recv_sem=in_recv.at[p, d],
            device_id={"lon": to(d)},
            device_id_type=MESH,
        )

    def outward(p, d):
        return pltpu.make_async_remote_copy(
            src_ref=state.at[pl.ds(to(d) * group, group), :, rows_of(p), :],
            dst_ref=out_ref.at[:, :, rows_of(p), columns(me)],
            send_sem=out_send.at[p, d],
            recv_sem=out_recv.at[p, d],
            device_id={"lon": to(d)},
            device_id_type=MESH,
        )

    def kept(p):
        return pltpu.make_async_copy(
            state.at[pl.ds(me * group, group), :, rows_of(p), :],
            out_ref.at[:, :, rows_of(p), columns(me)],
            own_sem.at[p],
        )

    def informing(d):
        return pltpu.make_async_remote_copy(
            src_ref=about_ref,
            dst_ref=info_all.at[me],
            send_sem=info_send.at[d],
            recv_sem=info_recv.at[d],
            device_id={"lon": to(d)},
            device_id_type=MESH,
        )

    def picking(d):
        return pltpu.make_async_remote_copy(
            src_ref=pick.at[to(d)],
            dst_ref=prior_parts.at[me],
            send_sem=pick_send.at[d],
            recv_sem=pick_recv.at[d],
            device_id={"lon": to(d)},
            device_id_type=MESH,
        )

    def lon_share(batch, side):
        shift = 2 * side - 1
        return pltpu.make_async_remote_copy(
            src_ref=folded.at[batch],
            dst_ref=landed.at[batch, side],
            send_sem=near_send.at[batch, side],
            recv_sem=near_recv.at[batch, side],
            device_id={"lon": lax.rem(me + shift + parts, parts)},
            device_id_type=MESH,
        )

    def lat_share(batch, side):
        shift = 2 * side - 1
        return pltpu.make_async_remote_copy(
            src_ref=table.at[batch, pl.ds(third, third), :],
            dst_ref=table.at[batch, pl.ds((1 - shift) * third, third), :],
            send_sem=near_send.at[batch, 2 + side],
            recv_sem=near_recv.at[batch, 2 + side],
            device_id={"lat": lax.rem(band + shift + bands, bands)},
            device_id_type=MESH,
        )

    barrier = pltpu.get_barrier_semaphore()
    for d in range(parts - 1, 0, -1):
        pl.semaphore_signal(barrier, inc=1, device_id={"lon": to(d)}, device_id_type=MESH)
    for shift in (-1, 1):
        beside = lax.rem(band + shift + bands, bands)
        pl.semaphore_signal(barrier, inc=1, device_id={"lat": beside}, device_id_type=MESH)
    fetched = [pltpu.make_async_copy(count_ref, counts, small_sem.at[5])]
    fetched[0].start()
    for i, ref in enumerate((row_ref, col_ref, value_ref, error_ref, weight_ref)):
        fetched.append(pltpu.make_async_copy(ref, small[i], small_sem.at[i]))
        fetched[-1].start()
    whole = pltpu.make_async_copy(members_ref, mem, own_sem.at[pieces])
    whole.start()
    own = pltpu.make_async_copy(
        members_ref.at[:, :, :, columns(me)], state.at[pl.ds(me * group, group)], own_sem.at[pieces + 1]
    )
    own.start()

    info_ref[...] = jnp.zeros_like(info_ref)
    for copy in fetched:
        copy.wait()
    spot = lax.broadcasted_iota(jnp.int32, (1, slots), 1)
    for batch in range(NBATCH):
        here = slice(batch * slots, (batch + 1) * slots)
        for i in range(4):
            info_ref[i : i + 1, here] = small[i][batch, 0].astype(jnp.float32)
        info_ref[4 : 4 + levels, here] = small[4][batch, 0, 0]
        info_ref[4 + levels : 5 + levels, here] = jnp.where(spot < counts[batch], 1.0, 0.0)
    about_ref[:2, :] = info_ref[:2, :]
    about_ref[2:, :] = info_ref[4 : 4 + levels, :]
    pl.semaphore_wait(barrier, parts - 1 + 2)

    for d in range(parts - 1, 0, -1):
        informing(d).start()

    def send_in(unit):
        for d in halves[unit % 2]:
            inward(unit // 2, d).start()

    def send_more(stage):
        first = sum(ISSUE[:stage])
        for unit in range(first, min(first + ISSUE[stage], 2 * pieces)):
            send_in(unit)

    send_more(0)

    for d in range(1, parts):
        informing(d).wait()
    info_all[me] = about_ref[...]
    whole.wait()
    cell = lax.broadcasted_iota(jnp.int32, (clon, LANES), 0).astype(jnp.float32)
    grid_row = lax.broadcasted_iota(jnp.int32, (clat, LANES), 0).astype(jnp.float32)

    def pick_for(sector):
        about = info_all[sector]
        hot = jnp.where(cell == about[1:2], 1.0, 0.0).astype(jnp.bfloat16)
        chosen = grid_row == about[0:1]
        weight = jnp.stack([jnp.where(chosen, about[2 + l : 3 + l], 0.0) for l in range(levels)], axis=0)
        for k in range(group):
            values = mem[k, :, :, columns(sector)].reshape(levels * clat, clon)
            high, low = split(values)
            rest = values - high.astype(jnp.float32) - low.astype(jnp.float32)
            found = jnp.dot(
                jnp.concatenate([high, low, rest.astype(jnp.bfloat16)], axis=1),
                jnp.concatenate([hot, hot, hot], axis=0),
                preferred_element_type=jnp.float32,
            ).reshape(levels, clat, LANES)
            pick[sector, k : k + 1, :] = jnp.sum(
                jnp.sum(found * weight, axis=0), axis=0, keepdims=True
            )

    def pick_other(d, carry):
        pick_for(to(parts - d))
        picking(parts - d).start()
        return carry

    lax.fori_loop(1, parts, pick_other, 0)
    send_more(1)
    pick_for(me)
    prior_parts[me] = pick[me]
    for d in range(1, parts):
        picking(d).wait()
    for i in range(parts):
        prior[i * group : (i + 1) * group, :] = prior_parts[i]

    cross[...] = jnp.zeros_like(cross)
    pack[...] = jnp.zeros_like(pack)
    opened[...] = jnp.zeros_like(opened)
    for batch in range(NBATCH):
        table[batch, total:, :] = jnp.zeros((table.shape[1] - total, LANES), jnp.float32)
    own_lat = lat_first + info_ref[0:1, :]
    own_lon = lon_first + info_ref[1:2, :]

    def share(batch):
        points = prior[...]
        mean = jnp.mean(points, axis=0, keepdims=True)
        pert = points - mean
        spread = jnp.sum(pert * pert, axis=0, keepdims=True) / (full - 1.0)
        err = info_ref[3:4, :]
        valid = info_ref[4 + levels : 5 + levels, :]
        denom = spread + err
        pack[:full, :] = pert
        pack[mine : mine + 1, :] = valid * (info_ref[2:3, :] - mean) / denom
        pack[mine + 1 : mine + 2, :] = valid / (denom * (1.0 + jnp.sqrt(err / denom)))
        pack[mine + 2 : mine + 3, :] = own_lat
        pack[mine + 3 : mine + 4, :] = own_lon
        if batch == 0:
            cross[:full, :] = pert
        fold = folded.shape[1]
        upper, lower = pack[:fold, :], pack[fold : 2 * fold, :]
        if batch == 0:
            lower = pltpu.roll(lower, slots, 1)
        else:
            upper = pltpu.roll(upper, slots, 1)
        folded[batch] = jnp.where(lax.broadcasted_iota(jnp.int32, upper.shape, 1) < slots, upper, lower)
        for side in range(2):
            lon_share(batch, side).start()
        send_more(2 + 2 * batch)
        turned = pack[...].T
        table[batch, 4 * slots : 5 * slots, :] = turned[batch * slots : (batch + 1) * slots]
        for side in range(2):
            lon_share(batch, side).wait()
            opened[:fold, :] = landed[batch, side]
            opened[fold : 2 * fold, :] = pltpu.roll(landed[batch, side], slots, 1)
            spot = 5 - 2 * side
            table[batch, spot * slots : (spot + 1) * slots, :] = opened[...].T[:slots]
        for side in range(2):
            lat_share(batch, side).start()
        send_more(3 + 2 * batch)
        for side in range(2):
            lat_share(batch, side).wait()

    lane = lax.broadcasted_iota(jnp.int32, (total, LANES), 1)
    cell_lon = lon_first + lax.broadcasted_iota(jnp.int32, (1, clon), 1).astype(jnp.float32)

    def prepare(batch):
        rows = table[batch, :total, :]
        lats[batch] = jnp.broadcast_to(rows[:, mine + 2 : mine + 3] - lat_first, (total, clon))
        dx = wrapped(cell_lon - rows[:, mine + 3 : mine + 4], 1.0 * nlon)
        gaps[batch] = dx * dx
        high, low = split(rows * (1.0 / (full - 1.0)))
        high = high.astype(jnp.float32)
        turned = pltpu.roll(low.astype(jnp.float32), full, 1)
        first = jnp.where(lane < full, high, turned)
        spill = 2 * full - LANES
        second = jnp.where(lane < spill, turned, pltpu.roll(high, spill, 1))
        priors[batch, :, :LANES] = first.astype(jnp.bfloat16)
        priors[batch, :, LANES:] = second.astype(jnp.bfloat16)[:, : 3 * full - LANES]
        for i in range(coef_t.shape[1] // LANES):
            block = table[batch, i * LANES : (i + 1) * LANES, :]
            turned = (block[:, mine : mine + 1] - block[:, mine + 1 : mine + 2] * block).T
            coef_t[:, i * LANES : (i + 1) * LANES] = turned[:full]
        high, low = split(coef_t[:, :total])
        coefs[batch, :full, :] = high
        coefs[batch, full:, :] = low
        for i in range(2 * third // LANES):
            block = table[batch, third + i * LANES : third + (i + 1) * LANES, :]
            turned = (block[:, mine : mine + 1] - block[:, mine + 1 : mine + 2] * block).T
            high, low = split(turned[:full])
            coefs_high[batch, :full, i * LANES : (i + 1) * LANES] = high
            coefs_high[batch, full:, i * LANES : (i + 1) * LANES] = low

    share(0)
    prepare(0)
    rows = table[0]
    cov = jnp.dot(rows, cross[...], precision=HIGHEST, preferred_element_type=jnp.float32) * (1.0 / (full - 1.0))
    dy = own_lat - rows[:, mine + 2 : mine + 3]
    dx = wrapped(own_lon - rows[:, mine + 3 : mine + 4], 1.0 * nlon)
    gain = cov * gaspari_sq(dx * dx + dy * dy)
    prior[...] = prior[...] + jnp.dot(coef_t[...], gain, precision=HIGHEST, preferred_element_type=jnp.float32)
    share(1)
    send_more(6)
    prepare(1)
    own.wait()

    state_flat = state.reshape(full * levels * clat, clon)

    def update(lo, hi, coef_ref, y):
        cell_lat = y.astype(jnp.float32)
        spots = [pl.ds(l * clat + y, full, stride=levels * clat) for l in range(levels)]
        value = jnp.concatenate([state_flat[spot, :] for spot in spots], axis=1)
        for batch in range(NBATCH):
            dy = lats[batch, lo:hi, :] - cell_lat
            taper = gaspari_sq(gaps[batch, lo:hi, :] + dy * dy)
            pert = value - jnp.mean(value, axis=0, keepdims=True)
            high, low = split(pert)
            stacked = jnp.concatenate([high, high, low], axis=0)
            cov = jnp.dot(priors[batch, lo:hi, :], stacked, preferred_element_type=jnp.float32)
            ghigh, glow = split(cov * jnp.concatenate([taper] * levels, axis=1))
            both = jnp.dot(coef_ref[batch, :, : hi - lo], ghigh, preferred_element_type=jnp.float32)
            rest = jnp.dot(coef_ref[batch, :full, : hi - lo], glow, preferred_element_type=jnp.float32)
            value = value + (both[:full] + (both[full:] + rest))
        for l, spot in enumerate(spots):
            state_flat[spot, :] = value[:, l * clon : (l + 1) * clon]

    kinds = []
    for p in range(pieces):
        lo = 0 if p * STEP + 1 < RAD else third
        hi = total if clat - (p * STEP + STEP - 1) < RAD else 2 * third
        if kinds and kinds[-1][2:] == (lo, hi):
            kinds[-1] = (kinds[-1][0], p + 1, lo, hi)
        else:
            kinds.append((p, p + 1, lo, hi))

    for begin, end, lo, hi in kinds:

        def one_piece(p, carry):
            for d in range(1, parts):
                inward(p, d).wait_recv()

            def one_row(i, inner):
                update(lo, hi, coefs if lo == 0 else coefs_high, p * STEP + i)
                return inner

            lax.fori_loop(0, STEP, one_row, 0)
            for d in order:
                outward(p, d).start()
            kept(p).start()
            return carry

        lax.fori_loop(begin, end, one_piece, 0)

    def finish(p, carry):
        for d in range(1, parts):
            inward(p, d).wait_send()
        for d in range(1, parts):
            outward(p, d).wait()
        kept(p).wait()
        return carry

    lax.fori_loop(0, pieces, finish, 0)


def body(bands, parts, members, obs_row, obs_col, obs_value, obs_error, obs_weight, obs_count):
    group, levels, clat, nlon = members.shape
    full = group * parts
    clon = nlon // parts
    slots = obs_row.shape[-1]
    assert NBATCH * slots == LANES and clon == LANES and full + 4 <= LANES and LANES < 2 * full and 3 * full <= 2 * LANES
    assert parts & (parts - 1) == 0 and levels <= 3 and bands >= 3 and parts >= 4

    smalls = (obs_row, obs_col, obs_value, obs_error, obs_weight)
    fold = -(-(full + 4) // 16) * 8
    pieces = clat // STEP
    total = 9 * slots
    padded = -(-total // LANES) * LANES
    f32, bf16 = jnp.float32, jnp.bfloat16
    dma = pltpu.SemaphoreType.DMA
    return pl.pallas_call(
        functools.partial(fused_kernel, bands, parts, slots),
        out_shape=pltpu.VMEM(members.shape, f32),
        in_specs=[pl.BlockSpec(memory_space=pl.ANY)] * (len(smalls) + 2),
        out_specs=pl.BlockSpec(memory_space=pltpu.VMEM),
        scratch_shapes=[
            [pltpu.VMEM(v.shape, v.dtype) for v in smalls],
            pltpu.SMEM((NBATCH,), jnp.int32),
            pltpu.VMEM((8, LANES), f32),
            pltpu.VMEM((2 + levels, LANES), f32),
            pltpu.VMEM(members.shape, f32),
            pltpu.VMEM((full, levels, clat, clon), f32),
            pltpu.VMEM((parts, 2 + levels, LANES), f32),
            pltpu.VMEM((parts, group, LANES), f32),
            pltpu.VMEM((parts, group, LANES), f32),
            pltpu.VMEM((full, LANES), f32),
            pltpu.VMEM((LANES, LANES), f32),
            pltpu.VMEM((LANES, LANES), f32),
            pltpu.VMEM((LANES, LANES), f32),
            pltpu.VMEM((NBATCH, fold, LANES), f32),
            pltpu.VMEM((NBATCH, 2, fold, LANES), f32),
            pltpu.VMEM((NBATCH, padded, LANES), f32),
            pltpu.VMEM((full, padded), f32),
            pltpu.VMEM((NBATCH, total, clon), f32),
            pltpu.VMEM((NBATCH, total, clon), f32),
            pltpu.VMEM((NBATCH, total, 3 * full), bf16),
            pltpu.VMEM((NBATCH, 2 * full, total), bf16),
            pltpu.VMEM((NBATCH, 2 * full, 6 * slots), bf16),
            dma((pieces, parts)),
            dma((pieces, parts)),
            dma((pieces, parts)),
            dma((pieces, parts)),
            dma((parts,)),
            dma((parts,)),
            dma((parts,)),
            dma((parts,)),
            dma((NBATCH, 4)),
            dma((NBATCH, 4)),
            dma((pieces + 2,)),
            dma((len(smalls) + 1,)),
        ],
        compiler_params=pltpu.CompilerParams(collective_id=0, has_side_effects=True, vmem_limit_bytes=50 << 20),
    )(*smalls, obs_count.reshape(NBATCH), members)


def solution(mesh):
    placed = (
        P("lon", None, "lat", None),
        P(None, "lat", "lon", None),
        P(None, "lat", "lon", None),
        P(None, "lat", "lon", None),
        P(None, "lat", "lon", None),
        P(None, "lat", "lon", None, None),
        P(None, "lat", "lon"),
    )
    return jax.shard_map(
        functools.partial(body, mesh.shape["lat"], mesh.shape["lon"]),
        mesh=mesh,
        in_specs=placed,
        out_specs=P("lon", None, "lat", None),
        check_vma=False,
    )
```
